128 devices in a mesh: gx: 8 (over y, core), gy: 16 (over z, x).
Axes of the slice: x: 4, y: 4, z: 4, core: 2. Of those that a mesh axis runs over, the one named last changes fastest.
Arguments:
- atm_tracers: float32 [16, 72, 131072], P(None, None, ('gx', 'gy')), may hold values from -4 to 6
- vert_inverse: float32 [1024, 72, 72], P(('gx', 'gy')), may hold values from 0 to 2
- ocean_tracers: float32 [16, 4, 512, 1024], P(None, None, 'gy', 'gx'), may hold values from -4 to 6
- velocity: float32 [2, 512, 1024], P(None, 'gy', 'gx'), may hold values from -0.3 to 0.3
- land_mask: int32 [512, 1024], P('gy', 'gx'), may hold values 0 or 1
- intersections: int32 [3, 9216], P(None, ('gx', 'gy')), may hold values from -1 to 63, as said below
- regrid_weights: float32 [8192, 128, 128], P(('gx', 'gy')), may hold values from 0.001 to 0.006
Outputs:
- atm_new: float32 [16, 72, 131072], P(None, None, ('gx', 'gy'))
- ocean_new: float32 [16, 4, 512, 1024], P(None, None, 'gy', 'gx')
The draws below stay inside these ranges and needn't reach their ends.
Inputs may be any that keep to these rules, and one draw needn't show every extreme that they name: `intersections`: row 1 is -1 in empty slots, else an ocean block row below 32; row 0 is below 8 and row 2 below 64.
All inputs are finite; a program needn't handle non-finite values. No bound on the sum of `land_mask` on one device may be relied on, other than what follows from the above.
Results may differ from the reference program's by a relative error of at most 0.0003.
Values sent between devices are 32-bit elements; how exact they have to be, the bound alone decides.
A program may use at most 192 MiB of HBM per device.

```python
import math
import jax
import jax.numpy as jnp
from jax import lax

K = 16
LA = 72
OL = 4
BLK = 128
OY = 32
ACB = 8
CAP = 8
WSL = 64
NSUB = 4
NYO = 512
NXO = 1024
NBLK = 1024
NCOL = 131072
NPAIR = 9216
NW = 8192
N_GX = 8
N_GY = 16
DEVICES = 128


def draw_intersections(key, part):
    first, second, third, fourth = jax.random.split(key, 4)
    atm_slot = jax.random.randint(first, (NPAIR,), 0, ACB)
    ocean_row = jax.random.randint(second, (NPAIR,), 0, OY)
    empty_roll = jax.random.randint(third, (NPAIR,), 0, 10)
    ocean_row = jnp.where(empty_roll < 3, -1, ocean_row)
    weight_slot = jax.random.randint(fourth, (NPAIR,), 0, WSL)
    return jnp.stack([atm_slot, ocean_row, weight_slot], 0).astype(jnp.int32)


def draw_vert_inverse(key, part):
    first, second = jax.random.split(key)
    diagonal = jax.random.uniform(first, (NBLK, LA), jnp.float32, 0.5, 1.0)
    spread = jax.random.uniform(second, (NBLK, LA, LA), jnp.float32, 0.0, 0.8 / LA)
    identity = jnp.eye(LA, dtype=jnp.float32)
    return spread + diagonal[:, :, None] * identity[None]


def draw_atm_tracers(key, part):
    first, second = jax.random.split(jax.random.fold_in(key, 11))
    offset = jax.random.uniform(first, (K, 1, 1), jnp.float32, 0.5, 1.5)
    noise = jnp.clip(jax.random.normal(second, (K, LA, NCOL), jnp.float32), -4.5, 4.5)
    return offset + noise


def draw_ocean_tracers(key, part):
    first, second = jax.random.split(jax.random.fold_in(key, 12))
    offset = jax.random.uniform(first, (K, 1, 1, 1), jnp.float32, 0.5, 1.5)
    noise = jnp.clip(jax.random.normal(second, (K, OL, NYO, NXO), jnp.float32), -4.5, 4.5)
    return offset + noise


def place_ends(values, stream_key, smallest, largest):
    extent = values.shape
    spot = [jax.random.randint(jax.random.fold_in(stream_key, axis), (), 0, extent[axis]) for axis in range(len(extent))]
    values = values.at[tuple(spot)].set(smallest)
    longest = extent.index(max(extent))
    spot[longest] = (spot[longest] + 1) % extent[longest]
    return values.at[tuple(spot)].set(largest)


def block_scale(stream_key, shape, shards, low, largest):
    level, own = 1.0, jax.random.fold_in(stream_key, 6)
    for axis_at, parts in shards:
        heights = jnp.exp(jax.random.uniform(jax.random.fold_in(own, axis_at), (parts,), jnp.float32, low / len(shards), largest / len(shards)))
        level = level * jnp.repeat(heights, shape[axis_at] // parts).reshape([-1 if axis == axis_at else 1 for axis in range(len(shape))])
    return level


def setup_inputs(seed: int = 0) -> dict:
    key_list = jax.random.split(jax.random.key(seed), 8)
    atm_tracers = draw_atm_tracers(jax.random.fold_in(key_list[7], 71), 0)
    vert_inverse = draw_vert_inverse(jax.random.fold_in(key_list[7], 71), 0)
    ocean_tracers = draw_ocean_tracers(jax.random.fold_in(key_list[7], 71), 0)
    velocity = jnp.clip(jax.random.uniform(key_list[3], (2, NYO, NXO), jnp.float32, -0.3, 0.3) * block_scale(key_list[3], (2, NYO, NXO), ((1, 16), (2, 8)), -0.4, 0.0), -0.3, 0.3)
    land_mask = place_ends((jax.random.randint(key_list[4], (NYO, NXO), 0, 4) < 3).astype(jnp.int32), jax.random.fold_in(key_list[4], 1), 0, 1)
    intersections = draw_intersections(jax.random.fold_in(key_list[7], 71), 0)
    regrid_weights = jnp.clip(jnp.exp(math.log(0.006) - 1.7917594 * jax.random.uniform(key_list[6], (NW, BLK, BLK), jnp.float32) ** block_scale(key_list[6], (NW, BLK, BLK), ((0, 128),), -0.2, 0.2)), 0.001, 0.006)
    return dict(atm_tracers=atm_tracers, vert_inverse=vert_inverse, ocean_tracers=ocean_tracers, velocity=velocity, land_mask=land_mask, intersections=intersections, regrid_weights=regrid_weights)


ocean_uptake = 0.5
air_uptake = 0.5
mix_horizontal = 0.15
mix_vertical = 0.2


def reference(atm_tracers, vert_inverse, ocean_tracers, velocity, land_mask, intersections, regrid_weights):
    highest = lax.Precision.HIGHEST
    slot_total = 9 * CAP
    wet_cells = land_mask.astype(jnp.float32)
    ocean_top = ocean_tracers[:, 0]
    atm_surface = atm_tracers[:, 0, :]
    atm_blocks = atm_surface.reshape(K, NBLK, BLK).transpose(1, 0, 2)
    surface_ext = jnp.concatenate([ocean_top * wet_cells, wet_cells[None]], 0)
    ext_blocks = surface_ext.reshape(K + 1, NYO * N_GX, BLK)
    groups = jnp.arange(slot_total, dtype=jnp.int32) // CAP
    shift_rows = groups // 3 - 1
    shift_cols = groups % 3 - 1

    def per_device(device):
        col_index = device // N_GY
        row_index = device % N_GY
        entries = lax.dynamic_slice_in_dim(intersections, (device * slot_total).astype(jnp.int32), slot_total, 1)
        atm_slot = entries[0]
        ocean_row = entries[1]
        weight_slot = entries[2]
        is_valid = ocean_row >= 0
        table = lax.dynamic_slice_in_dim(regrid_weights, (device * WSL).astype(jnp.int32), WSL, 0)
        weights = table[weight_slot]
        own_blocks = lax.dynamic_slice_in_dim(atm_blocks, (device * ACB).astype(jnp.int32), ACB, 0)[atm_slot]
        contrib = jnp.einsum("eka,eca->ekc", own_blocks, weights, precision=highest)
        target_row = ((row_index + shift_rows) % N_GY) * OY + jnp.maximum(ocean_row, 0)
        target_col = (col_index + shift_cols) % N_GX
        block_id = (target_row * N_GX + target_col).astype(jnp.int32)
        targets = jnp.where(is_valid, block_id, NYO * N_GX).astype(jnp.int32)
        picked = ext_blocks[:, jnp.where(is_valid, block_id, 0).astype(jnp.int32)]
        returned = jnp.einsum("kec,eca->eka", picked, weights, precision=highest)
        onehot = ((atm_slot[:, None] == jnp.arange(ACB, dtype=jnp.int32)[None, :]) & is_valid[:, None]).astype(jnp.float32)
        gathered = jnp.einsum("eb,eka->kba", onehot, returned, precision=highest)
        return contrib, targets, gathered

    contribs, targets, gathered = lax.map(per_device, jnp.arange(DEVICES, dtype=jnp.int32))
    summed = jax.ops.segment_sum(contribs.reshape(-1, K, BLK), targets.reshape(-1), num_segments=NYO * N_GX + 1)[:-1]
    ocean_in = summed.reshape(NYO, N_GX, K, BLK).transpose(2, 0, 1, 3).reshape(K, NYO, NXO)
    atm_in = gathered.transpose(1, 0, 2, 3).reshape(K + 1, NCOL)

    bottom = atm_surface + air_uptake * (atm_in[:K] - atm_in[K][None] * atm_surface)
    column_state = atm_tracers.at[:, 0, :].set(bottom).reshape(K, LA, NBLK, BLK)
    atm_new = jnp.einsum("bij,kjbc->kibc", vert_inverse, column_state, precision=highest).reshape(K, LA, NCOL)

    new_top = ocean_top + ocean_uptake * wet_cells * (ocean_in - ocean_top)
    tracer = ocean_tracers.at[:, 0].set(new_top) * wet_cells
    east_speed = velocity[0]
    north_speed = velocity[1]
    for substep in range(NSUB):
        east_cells = jnp.roll(tracer, -1, axis=3)
        west_cells = jnp.roll(tracer, 1, axis=3)
        north_cells = jnp.roll(tracer, -1, axis=2)
        south_cells = jnp.roll(tracer, 1, axis=2)
        tendency = -0.5 * east_speed * (east_cells - west_cells) - 0.5 * north_speed * (north_cells - south_cells)
        tendency = tendency + mix_horizontal * (east_cells + west_cells + north_cells + south_cells - 4.0 * tracer)
        above_level = jnp.concatenate([tracer[:, :1], tracer[:, :-1]], 1)
        below_level = jnp.concatenate([tracer[:, 1:], tracer[:, -1:]], 1)
        tracer = wet_cells * (tracer + tendency + mix_vertical * (above_level + below_level - 2.0 * tracer))
    return atm_new, tracer
```

```python
import functools

import jax
import jax.numpy as jnp
from jax import lax
from jax.experimental import pallas as pl
from jax.experimental.pallas import tpu as pltpu
from jax.sharding import PartitionSpec as P

K = 16
LA = 72
OL = 4
OY = 32
BLK = 128
ACB = 8
CAP = 8
WSL = 64
NSUB = 4
SLOTS = 9 * CAP
HW = NSUB
EXT_ROWS = OY + 2 * HW
EXT_COLS = 2 * BLK

ocean_uptake = 0.5
air_uptake = 0.5
mix_horizontal = 0.15
mix_vertical = 0.2

F32 = jnp.float32
BF16 = jnp.bfloat16
MESH = pl.DeviceIdType.MESH
NEIGHBOURS = (0, 8, 1, 7, 2, 6, 3, 5)
REQUEST, CONTRIB, SURFACE, EARLY, LATE = range(5)
NQ = 4
EARLY_ROWS = NQ * 48 + 16
EARLY_STRIP = NQ * 16


def split2(x):
    hi = x.astype(BF16)
    return hi, (x - hi.astype(F32)).astype(BF16)


def split3(x):
    hi = x.astype(BF16)
    rest = x - hi.astype(F32)
    mid = rest.astype(BF16)
    return hi, mid, (rest - mid.astype(F32)).astype(BF16)


def dot(a, b):
    return jnp.dot(a, b, preferred_element_type=F32)


def dot_nt(a, b):
    return lax.dot_general(a, b, (((1,), (1,)), ((), ())), preferred_element_type=F32)


def exchange_kernel(
    inter, atm, oc, vel, mask, w_hbm,
    bottom, top, er_in, ec_in, es_in, lr_in, lc_in, ls_in,
    wbuf, abuf, ast, req, reqs, cbuf, cin, sbuf, sin, acc,
    er, ec, es, lr, lc, ls,
    wsem, asem, ssem, rsem,
):
    nx, ny = lax.axis_size("gx"), lax.axis_size("gy")
    i, j = lax.axis_index("gx"), lax.axis_index("gy")

    def device(g, sign):
        dy, dx = g // 3 - 1, g % 3 - 1
        return ((i + sign * dx + nx) % nx, (j + sign * dy + ny) % ny)

    def message(kind, g, src, dst, sign=1):
        return pltpu.make_async_remote_copy(
            src_ref=src, dst_ref=dst, send_sem=ssem.at[kind, g], recv_sem=rsem.at[kind, g],
            device_id=device(g, sign), device_id_type=MESH,
        )

    chunk = WSL // 8
    loads = [
        pltpu.make_async_copy(
            w_hbm.at[pl.ds(c * chunk, chunk)], wbuf.at[pl.ds(c * chunk, chunk)], wsem.at[c]
        )
        for c in range(8)
    ]
    surface_load = pltpu.make_async_copy(atm.at[:, pl.ds(0, 8), :], abuf, asem)
    surface_load.start()
    for load in loads:
        load.start()

    barrier = pltpu.get_barrier_semaphore()
    for g in NEIGHBOURS:
        pl.semaphore_signal(barrier, inc=1, device_id=device(g, 1), device_id_type=MESH)

    for e in range(SLOTS):
        req[e // CAP, pl.ds(e % CAP, 1), :] = jnp.full((1, BLK), inter[1, e], jnp.int32)
    reqs[4] = req[4]
    wet = mask[...].astype(F32)

    er[...] = jnp.zeros_like(er)
    es[...] = jnp.zeros_like(es)
    for q in range(NQ):
        for lev in range(1, OL):
            for p in range(4):
                row = q * 48 + (lev - 1) * 16 + p * 4
                er[0, row:row + HW, :] = oc[4 * q + p, lev, 0:HW, :]
                er[1, row:row + HW, :] = oc[4 * q + p, lev, OY - HW:OY, :]
    for n in range(3):
        row = NQ * 48 + n * 4
        field = vel[n] if n < 2 else wet
        er[0, row:row + HW, :] = field[0:HW]
        er[1, row:row + HW, :] = field[OY - HW:OY]
    for q in range(NQ):
        for lev in range(1, OL):
            turned = oc[4 * q:4 * q + 4, lev].reshape(BLK, BLK).T
            row = q * 16 + (lev - 1) * 4
            es[0, row:row + HW, :] = turned[0:HW]
            es[1, row:row + HW, :] = turned[BLK - HW:BLK]
    turned = jnp.concatenate([vel[0], vel[1], wet, jnp.zeros_like(wet)], 0).T
    es[0, 12:16, :] = turned[0:HW]
    es[1, 12:16, :] = turned[BLK - HW:BLK]
    for side in range(2):
        for blk in range(2):
            turned = er[side, blk * BLK:(blk + 1) * BLK, :].T
            ec[2 * side, blk * HW:(blk + 1) * HW, :] = turned[0:HW]
            ec[2 * side + 1, blk * HW:(blk + 1) * HW, :] = turned[BLK - HW:BLK]

    pl.semaphore_wait(barrier, len(NEIGHBOURS))

    requests = [message(REQUEST, g, req.at[g], reqs.at[g]) for g in NEIGHBOURS]
    for copy in requests:
        copy.start()

    sides = {1: 0, 7: 1}
    ends = {3: 0, 5: 1}
    corners = {0: 0, 2: 1, 6: 2, 8: 3}

    def halo(kind, rows, corner, strip, rows_in, corner_in, strip_in, count):
        copies = []
        for g in NEIGHBOURS:
            if g in sides:
                n = sides[g]
                copies.append(message(kind, g, rows.at[n, pl.ds(0, count)], rows_in.at[n]))
            elif g in ends:
                n = ends[g]
                copies.append(message(kind, g, strip.at[n], strip_in.at[n]))
            else:
                n = corners[g]
                copies.append(message(kind, g, corner.at[n], corner_in.at[n]))
        return copies

    early = halo(EARLY, er, ec, es, er_in, ec_in, es_in, EARLY_ROWS)
    for copy in early:
        copy.start()

    surface_load.wait()
    for b in range(ACB):
        block = abuf[:, 0, b * BLK:(b + 1) * BLK]
        hi, lo = split2(block)
        ast[b, 0:K, :] = hi
        ast[b, K:2 * K, :] = lo
    for load in loads:
        load.wait()

    def contrib_group(t, carry):
        g = (t // 2) * (1 - t % 2) + (8 - t // 2) * (t % 2)
        for s in range(CAP):
            e = g * CAP + s
            hi, lo = split2(wbuf[jnp.maximum(inter[2, e], 0)])
            a = ast[jnp.maximum(inter[0, e], 0)]
            first = dot_nt(a, hi)
            second = dot_nt(a[0:K], lo)
            cbuf[g, pl.ds(s, K, stride=CAP), :] = first[0:K] + first[K:2 * K] + second

        @pl.when(g != 4)
        def _():
            message(CONTRIB, g, cbuf.at[g], cin.at[g]).start()

        return carry

    lax.fori_loop(0, 9, contrib_group, 0)
    cin[4] = cbuf[4]

    for copy in requests:
        copy.wait_recv()
    lanes = lax.broadcasted_iota(jnp.int32, (SLOTS, BLK), 1)
    chosen = (reqs[...].reshape(SLOTS, BLK) == lanes).astype(F32)
    pick = chosen[:, 0:OY].astype(BF16)
    for k in range(0, K, 2):
        pair = jnp.concatenate([oc[k, 0] * wet, oc[k + 1, 0] * wet], 1)
        hi, mid, lo = split3(pair)
        rows = dot(pick, hi) + dot(pick, mid) + dot(pick, lo)
        for g in range(9):
            sbuf[g, k * CAP:(k + 1) * CAP, :] = rows[g * CAP:(g + 1) * CAP, 0:BLK]
            sbuf[g, (k + 1) * CAP:(k + 2) * CAP, :] = rows[g * CAP:(g + 1) * CAP, BLK:2 * BLK]
    rows = dot(pick, wet.astype(BF16))
    for g in range(9):
        sbuf[g, K * CAP:(K + 1) * CAP, :] = rows[g * CAP:(g + 1) * CAP]
    sin[4] = sbuf[4]
    for g in NEIGHBOURS:
        message(SURFACE, g, sbuf.at[g], sin.at[g], -1).start()

    place = chosen.T[0:OY].astype(BF16)
    for g in NEIGHBOURS:
        message(CONTRIB, g, cbuf.at[g], cin.at[g]).wait_recv()
    lr[...] = jnp.zeros_like(lr)
    ls[...] = jnp.zeros_like(ls)
    lc[...] = jnp.zeros_like(lc)
    for k in range(0, K, 2):
        pair = jnp.concatenate(
            [cin[:, n * CAP:(n + 1) * CAP, :].reshape(SLOTS, BLK) for n in (k, k + 1)], 1
        )
        hi, mid, lo = split3(pair)
        arrived = dot(place, hi) + dot(place, mid) + dot(place, lo)
        for n in range(2):
            old = oc[k + n, 0]
            new = old + ocean_uptake * wet * (arrived[:, n * BLK:(n + 1) * BLK] - old)
            top[k + n] = new
            lr[0, (k + n) * 4:(k + n) * 4 + 4, :] = new[0:HW]
            lr[1, (k + n) * 4:(k + n) * 4 + 4, :] = new[OY - HW:OY]
    for q in range(NQ):
        turned = top[4 * q:4 * q + 4].reshape(BLK, BLK).T
        ls[0, q * 8:q * 8 + HW, :] = turned[0:HW]
        ls[1, q * 8:q * 8 + HW, :] = turned[BLK - HW:BLK]
    for side in range(2):
        turned = lr[side].T
        lc[2 * side, 0:HW, :] = turned[0:HW]
        lc[2 * side + 1, 0:HW, :] = turned[BLK - HW:BLK]
    late = halo(LATE, lr, lc, ls, lr_in, lc_in, ls_in, 4 * K)
    for copy in late:
        copy.start()

    acc[...] = jnp.zeros_like(acc)

    def return_group(t, carry):
        t = (t + 8) % 9
        g = (t // 2) * (1 - t % 2) + (8 - t // 2) * (t % 2)

        @pl.when(g != 4)
        def _():
            message(SURFACE, g, sbuf.at[g], sin.at[g], -1).wait_recv()

        parts = []
        for s in range(CAP):
            e = g * CAP + s
            hi, lo = split2(wbuf[jnp.maximum(inter[2, e], 0)])
            ahi, alo = split2(sin[g, pl.ds(s, K, stride=CAP), :])
            wets = jnp.broadcast_to(sin[g, pl.ds(K * CAP + s, 1), :], (K, BLK)).astype(BF16)
            lhs = jnp.concatenate([ahi, alo, wets], 0)
            first = dot(lhs, hi)
            second = dot(lhs, lo)
            parts.append((
                first[0:K] + first[K:2 * K] + second[0:K],
                first[2 * K:2 * K + 8] + second[2 * K:2 * K + 8],
            ))
        for b in range(ACB):
            tracers, wets = acc[b, 0:K, :], acc[b, K:K + 8, :]
            for s in range(CAP):
                e = g * CAP + s
                here = jnp.where((inter[0, e] == b) & (inter[1, e] >= 0), 1.0, 0.0).astype(F32)
                tracers = tracers + here * parts[s][0]
                wets = wets + here * parts[s][1]
            acc[b, 0:K, :] = tracers
            acc[b, K:K + 8, :] = wets
        return carry

    lax.fori_loop(0, 9, return_group, 0)
    for b in range(ACB):
        old = abuf[:, 0, b * BLK:(b + 1) * BLK]
        bottom[:, b * BLK:(b + 1) * BLK] = old + air_uptake * (
            acc[b, 0:K, :] - acc[b, K:K + 1, :] * old
        )

    for copy in requests:
        copy.wait_send()
    for copy in early:
        copy.wait()
    for copy in late:
        copy.wait()
    for g in NEIGHBOURS:
        message(CONTRIB, g, cbuf.at[g], cin.at[g]).wait_send()
        message(SURFACE, g, sbuf.at[g], sin.at[g], -1).wait_send()


def exchange(inter, atm, oc, vel, mask, weights):
    vmem = pl.BlockSpec(memory_space=pltpu.VMEM)
    shapes = [
        (K, ACB * BLK), (K, OY, BLK),
        (2, EARLY_ROWS, BLK), (4, 8, BLK), (2, EARLY_STRIP, BLK),
        (2, 4 * K, BLK), (4, 8, BLK), (2, 8 * NQ, BLK),
    ]
    return pl.pallas_call(
        exchange_kernel,
        out_shape=[jax.ShapeDtypeStruct(s, F32) for s in shapes],
        in_specs=[
            pl.BlockSpec(memory_space=pltpu.SMEM),
            pl.BlockSpec(memory_space=pl.ANY),
            vmem, vmem, vmem,
            pl.BlockSpec(memory_space=pl.ANY),
        ],
        out_specs=[vmem] * len(shapes),
        scratch_shapes=[
            pltpu.VMEM((WSL, BLK, BLK), F32),
            pltpu.VMEM((K, 8, ACB * BLK), F32),
            pltpu.VMEM((ACB, 2 * K, BLK), BF16),
            pltpu.VMEM((9, CAP, BLK), jnp.int32),
            pltpu.VMEM((9, CAP, BLK), jnp.int32),
            pltpu.VMEM((9, K * CAP, BLK), F32),
            pltpu.VMEM((9, K * CAP, BLK), F32),
            pltpu.VMEM((9, (K + 1) * CAP, BLK), F32),
            pltpu.VMEM((9, (K + 1) * CAP, BLK), F32),
            pltpu.VMEM((ACB, K + 8, BLK), F32),
            pltpu.VMEM((2, 2 * BLK, BLK), F32),
            pltpu.VMEM((4, 8, BLK), F32),
            pltpu.VMEM((2, EARLY_STRIP, BLK), F32),
            pltpu.VMEM((2, BLK, BLK), F32),
            pltpu.VMEM((4, 8, BLK), F32),
            pltpu.VMEM((2, 8 * NQ, BLK), F32),
            pltpu.SemaphoreType.DMA((8,)),
            pltpu.SemaphoreType.DMA,
            pltpu.SemaphoreType.DMA((5, 9)),
            pltpu.SemaphoreType.DMA((5, 9)),
        ],
        compiler_params=pltpu.CompilerParams(collective_id=0, has_side_effects=True),
        name="exchange",
    )(inter, atm, oc, vel, mask, weights)


def step_kernel(
    atm, mix, bottom, oc, top, vel, mask, er, ec, es, lr, lc, ls,
    atm_out, oc_out, coef, xs, ct,
):
    q = pl.program_id(0)

    def spread(east, west):
        gap = jnp.zeros((BLK - 2 * HW, BLK), F32)
        return jnp.concatenate([east, gap, west], 0).T

    @pl.when(q == 0)
    def _():
        for side in range(2):
            for blk in range(2):
                ct[side, blk * BLK:(blk + 1) * BLK, :] = spread(
                    ec[2 * side, blk * HW:(blk + 1) * HW, :],
                    ec[2 * side + 1, blk * HW:(blk + 1) * HW, :],
                )
            ct[side, 2 * BLK:3 * BLK, :] = spread(lc[2 * side, 0:HW, :], lc[2 * side + 1, 0:HW, :])
        ends = spread(es[0, 12:16, :], es[1, 12:16, :])
        fields = []
        for n in range(3):
            own = vel[n] if n < 2 else mask[...].astype(F32)
            row = NQ * 48 + n * 4
            left = jnp.concatenate([own, er[0, row:row + HW, :], er[1, row:row + HW, :]], 0)
            right = jnp.concatenate(
                [ends[n * OY:(n + 1) * OY], ct[0, row:row + HW, :], ct[1, row:row + HW, :]], 0
            )
            fields.append(jnp.concatenate([left, right], 1))
        u, v, wet = fields
        coef[0] = wet * (mix_horizontal - 0.5 * u)
        coef[1] = wet * (mix_horizontal + 0.5 * u)
        coef[2] = wet * (mix_horizontal - 0.5 * v)
        coef[3] = wet * (mix_horizontal + 0.5 * v)
        coef[4] = wet * mix_vertical
        coef[5] = wet * (1.0 - 4.0 * mix_horizontal - 2.0 * mix_vertical)
        coef[6] = wet

    for lev in range(OL):
        if lev == 0:
            base = pl.multiple_of(q * 16, 16)
            north, south = lr[0, pl.ds(base, 16), :], lr[1, pl.ds(base, 16), :]
            corner = pl.multiple_of(2 * BLK + q * 16, 16)
            group = pl.multiple_of(q * 8, 8)
            ends = spread(ls[0, pl.ds(group, 8), :][0:HW], ls[1, pl.ds(group, 8), :][0:HW])
        else:
            base = pl.multiple_of(q * 48 + (lev - 1) * 16, 16)
            north, south = er[0, pl.ds(base, 16), :], er[1, pl.ds(base, 16), :]
            corner = base
            group = pl.multiple_of(q * 16, 16)
            piece = slice((lev - 1) * HW, lev * HW)
            ends = spread(es[0, pl.ds(group, 16), :][piece], es[1, pl.ds(group, 16), :][piece])
        north_ends, south_ends = ct[0, pl.ds(corner, 16), :], ct[1, pl.ds(corner, 16), :]
        for p in range(4):
            part = slice(p * 4, p * 4 + 4)
            xs[p, lev, 0:OY, 0:BLK] = top[p] if lev == 0 else oc[p, lev]
            xs[p, lev, OY:OY + HW, 0:BLK] = north[part]
            xs[p, lev, OY + HW:EXT_ROWS, 0:BLK] = south[part]
            xs[p, lev, 0:OY, BLK:EXT_COLS] = ends[p * OY:(p + 1) * OY]
            xs[p, lev, OY:OY + HW, BLK:EXT_COLS] = north_ends[part]
            xs[p, lev, OY + HW:EXT_ROWS, BLK:EXT_COLS] = south_ends[part]

    def ocean(p, carry):
        levels = [xs[p, lev] * coef[6] for lev in range(OL)]
        for _ in range(NSUB):
            new = []
            for lev in range(OL):
                x = levels[lev]
                above, below = levels[max(lev - 1, 0)], levels[min(lev + 1, OL - 1)]
                new.append(
                    coef[0] * pltpu.roll(x, EXT_COLS - 1, 1)
                    + coef[1] * pltpu.roll(x, 1, 1)
                    + coef[2] * pltpu.roll(x, EXT_ROWS - 1, 0)
                    + coef[3] * pltpu.roll(x, 1, 0)
                    + coef[4] * (above + below)
                    + coef[5] * x
                )
            levels = new
        for lev in range(OL):
            oc_out[p, lev] = levels[lev][0:OY, 0:BLK]
        return carry

    lax.fori_loop(0, 4, ocean, 0)

    for b in range(2):
        m = jnp.concatenate([mix[b], jnp.zeros((LA, EXT_COLS - LA), F32)], 1)
        mh = m.astype(BF16).astype(F32)
        stacked = (mh + pltpu.roll(mh, 80, 1) + pltpu.roll(m - mh, 160, 1)).astype(BF16)
        first = lax.broadcasted_iota(jnp.int32, (8, BLK), 0) == 0
        cols = slice(b * BLK, (b + 1) * BLK)

        for k in range(0, K, 2):
            sides = []
            for n in (k, k + 1):
                surface = jnp.broadcast_to(bottom[n:n + 1, cols], (8, BLK))
                low = jnp.where(first, surface, atm[n, 0:8, cols])
                x = jnp.concatenate([low, atm[n, 8:LA, cols], jnp.zeros((8, BLK), F32)], 0)
                hi, lo = split2(x)
                sides.append(jnp.concatenate([hi, lo, hi, jnp.zeros((16, BLK), BF16)], 0))
            out = dot(stacked, jnp.concatenate(sides, 1))
            atm_out[k, :, cols] = out[:, 0:BLK]
            atm_out[k + 1, :, cols] = out[:, BLK:2 * BLK]


def local_step(atm, mix, bottom, oc, top, vel, mask, halos):
    vmem = pl.BlockSpec(memory_space=pltpu.VMEM)
    return pl.pallas_call(
        step_kernel,
        grid=(NQ,),
        out_shape=[
            jax.ShapeDtypeStruct(atm.shape, F32),
            jax.ShapeDtypeStruct(oc.shape, F32),
        ],
        in_specs=[
            pl.BlockSpec((K, LA, 2 * BLK), lambda q: (0, 0, q)),
            pl.BlockSpec((2, LA, LA), lambda q: (q, 0, 0)),
            pl.BlockSpec((K, 2 * BLK), lambda q: (0, q)),
            pl.BlockSpec((4, OL, OY, BLK), lambda q: (q, 0, 0, 0)),
            pl.BlockSpec((4, OY, BLK), lambda q: (q, 0, 0)),
        ] + [vmem] * 8,
        out_specs=[
            pl.BlockSpec((K, LA, 2 * BLK), lambda q: (0, 0, q)),
            pl.BlockSpec((4, OL, OY, BLK), lambda q: (q, 0, 0, 0)),
        ],
        scratch_shapes=[
            pltpu.VMEM((7, EXT_ROWS, EXT_COLS), F32),
            pltpu.VMEM((4, OL, EXT_ROWS, EXT_COLS), F32),
            pltpu.VMEM((2, 3 * BLK, BLK), F32),
        ],
        name="step",
    )(atm, mix, bottom, oc, top, vel, mask, *halos)


def body(atm, mix, oc, vel, mask, inter, weights):
    bottom, top, *halos = exchange(inter, atm, oc, vel, mask, weights)
    return tuple(local_step(atm, mix, bottom, oc, top, vel, mask, halos))


def solution(mesh):
    in_specs = (
        P(None, None, ("gx", "gy")),
        P(("gx", "gy"), None, None),
        P(None, None, "gy", "gx"),
        P(None, "gy", "gx"),
        P("gy", "gx"),
        P(None, ("gx", "gy")),
        P(("gx", "gy"), None, None),
    )
    out_specs = (P(None, None, ("gx", "gy")), P(None, None, "gy", "gx"))
    return jax.shard_map(body, mesh=mesh, in_specs=in_specs, out_specs=out_specs, check_vma=False)
```

```python
import functools

import jax
import jax.numpy as jnp
from jax import lax
from jax.experimental import pallas as pl
from jax.experimental.pallas import tpu as pltpu
from jax.sharding import PartitionSpec as P

K = 16
LA = 72
OL = 4
OY = 32
BLK = 128
ACB = 8
CAP = 8
WSL = 64
NSUB = 4
SLOTS = 9 * CAP
HW = NSUB
EXT_ROWS = OY + 2 * HW
EXT_COLS = 2 * BLK

ocean_uptake = 0.5
air_uptake = 0.5
mix_horizontal = 0.15
mix_vertical = 0.2

F32 = jnp.float32
BF16 = jnp.bfloat16
MESH = pl.DeviceIdType.MESH
NEIGHBOURS = (0, 8, 1, 7, 2, 6, 3, 5)
REQUEST, CONTRIB, SURFACE, EARLY, LATE = range(5)
NQ = 4
EARLY_ROWS = NQ * 48 + 16
EARLY_STRIP = NQ * 16


def split2(x):
    hi = x.astype(BF16)
    return hi, (x - hi.astype(F32)).astype(BF16)


def split3(x):
    hi = x.astype(BF16)
    rest = x - hi.astype(F32)
    mid = rest.astype(BF16)
    return hi, mid, (rest - mid.astype(F32)).astype(BF16)


def dot(a, b):
    return jnp.dot(a, b, preferred_element_type=F32)


def dot_nt(a, b):
    return lax.dot_general(a, b, (((1,), (1,)), ((), ())), preferred_element_type=F32)


def exchange_kernel(
    inter_hbm, atm_hbm, mix_hbm, oc_hbm, vel_hbm, mask_hbm, w_hbm,
    mixed, first_column, bottom, oc, fields, er_in, ec_in, es_in, lr_in, lc_in, ls_in,
    inter, wbuf, abuf, xbuf, mbuf, maskbuf, stacked, ast, req, reqs, cbuf, cin, sbuf, sin, acc,
    er, ec, es, lr, lc, ls,
    wsem, xsem, lsem, ssem, rsem,
):
    nx, ny = lax.axis_size("gx"), lax.axis_size("gy")
    i, j = lax.axis_index("gx"), lax.axis_index("gy")

    def device(g, sign):
        dy, dx = g // 3 - 1, g % 3 - 1
        return ((i + sign * dx + nx) % nx, (j + sign * dy + ny) % ny)

    def message(kind, g, src, dst, sign=1):
        return pltpu.make_async_remote_copy(
            src_ref=src, dst_ref=dst, send_sem=ssem.at[kind, g], recv_sem=rsem.at[kind, g],
            device_id=device(g, sign), device_id_type=MESH,
        )

    barrier = pltpu.get_barrier_semaphore()
    for g in NEIGHBOURS:
        pl.semaphore_signal(barrier, inc=1, device_id=device(g, 1), device_id_type=MESH)

    chunk = WSL // 8
    small = [
        pltpu.make_async_copy(src, dst, lsem.at[n])
        for n, (src, dst) in enumerate((
            (oc_hbm, oc), (vel_hbm, fields.at[pl.ds(0, 2)]), (mask_hbm, maskbuf),
            (atm_hbm.at[:, pl.ds(0, 8), :], abuf), (mix_hbm, mbuf), (inter_hbm, inter),
        ))
    ]
    loads = [
        pltpu.make_async_copy(
            w_hbm.at[pl.ds(c * chunk, chunk)], wbuf.at[pl.ds(c * chunk, chunk)], wsem.at[c]
        )
        for c in range(8)
    ]
    columns = [
        pltpu.make_async_copy(atm_hbm.at[pl.ds(2 * c, 2)], xbuf.at[pl.ds(2 * c, 2)], xsem.at[c])
        for c in range(8)
    ]
    for load in small[5:6] + small[0:5] + loads:
        load.start()

    small[5].wait()
    for e in range(SLOTS):
        req[e // CAP, pl.ds(e % CAP, 1), :] = jnp.full((1, BLK), inter[1, e], jnp.int32)
    reqs[4] = req[4]
    for load in small[0:3]:
        load.wait()
    wet = maskbuf[...].astype(F32)
    fields[2] = wet
    vel = fields

    er[:, NQ * 48:2 * BLK, :] = jnp.zeros((2, 2 * BLK - NQ * 48, BLK), F32)
    es[...] = jnp.zeros_like(es)
    for q in range(NQ):
        for lev in range(1, OL):
            for p in range(4):
                row = q * 48 + (lev - 1) * 16 + p * 4
                er[0, row:row + HW, :] = oc[4 * q + p, lev, 0:HW, :]
                er[1, row:row + HW, :] = oc[4 * q + p, lev, OY - HW:OY, :]
    for n in range(3):
        row = NQ * 48 + n * 4
        field = vel[n] if n < 2 else wet
        er[0, row:row + HW, :] = field[0:HW]
        er[1, row:row + HW, :] = field[OY - HW:OY]
    for q in range(NQ):
        for lev in range(1, OL):
            turned = oc[4 * q:4 * q + 4, lev].reshape(BLK, BLK).T
            row = q * 16 + (lev - 1) * 4
            es[0, row:row + HW, :] = turned[0:HW]
            es[1, row:row + HW, :] = turned[BLK - HW:BLK]
    turned = jnp.concatenate([vel[0], vel[1], wet, jnp.zeros_like(wet)], 0).T
    es[0, 12:16, :] = turned[0:HW]
    es[1, 12:16, :] = turned[BLK - HW:BLK]
    for side in range(2):
        for blk in range(2):
            turned = er[side, blk * BLK:(blk + 1) * BLK, :].T
            ec[2 * side, blk * HW:(blk + 1) * HW, :] = turned[0:HW]
            ec[2 * side + 1, blk * HW:(blk + 1) * HW, :] = turned[BLK - HW:BLK]

    pl.semaphore_wait(barrier, len(NEIGHBOURS))

    requests = [message(REQUEST, g, req.at[g], reqs.at[g]) for g in NEIGHBOURS]
    for copy in requests:
        copy.start()

    sides = {1: 0, 7: 1}
    ends = {3: 0, 5: 1}
    corners = {0: 0, 2: 1, 6: 2, 8: 3}

    def halo(kind, rows, corner, strip, rows_in, corner_in, strip_in, count):
        copies = []
        for g in NEIGHBOURS:
            if g in sides:
                n = sides[g]
                copies.append(message(kind, g, rows.at[n, pl.ds(0, count)], rows_in.at[n]))
            elif g in ends:
                n = ends[g]
                copies.append(message(kind, g, strip.at[n], strip_in.at[n]))
            else:
                n = corners[g]
                copies.append(message(kind, g, corner.at[n], corner_in.at[n]))
        return copies

    early = halo(EARLY, er, ec, es, er_in, ec_in, es_in, EARLY_ROWS)
    for copy in early:
        copy.start()

    small[3].wait()
    for b in range(ACB):
        block = abuf[:, 0, b * BLK:(b + 1) * BLK]
        hi, lo = split2(block)
        ast[b, 0:K, :] = hi
        ast[b, K:2 * K, :] = lo
    for load in loads:
        load.wait()
    for load in columns:
        load.start()

    def contrib_group(t, carry):
        g = (t // 2) * (1 - t % 2) + (8 - t // 2) * (t % 2)
        for s in range(CAP):
            e = g * CAP + s
            hi, lo = split2(wbuf[jnp.maximum(inter[2, e], 0)])
            a = ast[jnp.maximum(inter[0, e], 0)]
            first = dot_nt(a, hi)
            second = dot_nt(a[0:K], lo)
            cbuf[g, pl.ds(s, K, stride=CAP), :] = first[0:K] + first[K:2 * K] + second

        @pl.when(g != 4)
        def _():
            message(CONTRIB, g, cbuf.at[g], cin.at[g]).start()

        return carry

    lax.fori_loop(0, 9, contrib_group, 0)
    cin[4] = cbuf[4]

    for copy in requests:
        copy.wait_recv()
    lanes = lax.broadcasted_iota(jnp.int32, (SLOTS, BLK), 1)
    chosen = (reqs[...].reshape(SLOTS, BLK) == lanes).astype(F32)
    pick = chosen[:, 0:OY].astype(BF16)
    for k in range(0, K, 2):
        pair = jnp.concatenate([oc[k, 0] * wet, oc[k + 1, 0] * wet], 1)
        hi, mid, lo = split3(pair)
        rows = dot(pick, hi) + dot(pick, mid) + dot(pick, lo)
        for g in range(9):
            sbuf[g, k * CAP:(k + 1) * CAP, :] = rows[g * CAP:(g + 1) * CAP, 0:BLK]
            sbuf[g, (k + 1) * CAP:(k + 2) * CAP, :] = rows[g * CAP:(g + 1) * CAP, BLK:2 * BLK]
    rows = dot(pick, wet.astype(BF16))
    for g in range(9):
        sbuf[g, K * CAP:(K + 1) * CAP, :] = rows[g * CAP:(g + 1) * CAP]
    sin[4] = sbuf[4]
    for g in NEIGHBOURS:
        message(SURFACE, g, sbuf.at[g], sin.at[g], -1).start()

    small[4].wait()
    for b in range(ACB):
        m = jnp.concatenate([mbuf[b], jnp.zeros((LA, 2 * BLK - LA), F32)], 1)
        first_column[b] = jnp.broadcast_to(m[:, 0:1], (LA, BLK))
        mh = m.astype(BF16).astype(F32)
        stacked[b] = (mh + pltpu.roll(mh, 80, 1) + pltpu.roll(m - mh, 160, 1)).astype(BF16)
    upper = lax.broadcasted_iota(jnp.int32, (8, BLK), 0) > 0

    for c in range(8):
        columns[c].wait()

    def mixing(c, carry):
        for b in range(ACB):
            cols = slice(b * BLK, (b + 1) * BLK)
            sides = []
            for n in range(2):
                x = jnp.concatenate([
                    jnp.where(upper, xbuf[2 * c + n, 0:8, cols], 0.0),
                    xbuf[2 * c + n, 8:LA, cols],
                    jnp.zeros((8, BLK), F32),
                ], 0)
                hi, lo = split2(x)
                sides.append(jnp.concatenate([hi, lo, hi, jnp.zeros((16, BLK), BF16)], 0))
            out = dot(stacked[b], jnp.concatenate(sides, 1))
            mixed[2 * c, :, cols] = out[:, 0:BLK]
            mixed[2 * c + 1, :, cols] = out[:, BLK:2 * BLK]
        return carry

    lax.fori_loop(0, 8, mixing, 0)

    place = chosen.T[0:OY].astype(BF16)
    for g in NEIGHBOURS:
        message(CONTRIB, g, cbuf.at[g], cin.at[g]).wait_recv()
    lr[...] = jnp.zeros_like(lr)
    ls[...] = jnp.zeros_like(ls)
    lc[...] = jnp.zeros_like(lc)
    for k in range(0, K, 2):
        pair = jnp.concatenate(
            [cin[:, n * CAP:(n + 1) * CAP, :].reshape(SLOTS, BLK) for n in (k, k + 1)], 1
        )
        hi, mid, lo = split3(pair)
        arrived = dot(place, hi) + dot(place, mid) + dot(place, lo)
        for n in range(2):
            old = oc[k + n, 0]
            new = old + ocean_uptake * wet * (arrived[:, n * BLK:(n + 1) * BLK] - old)
            oc[k + n, 0] = new
            lr[0, (k + n) * 4:(k + n) * 4 + 4, :] = new[0:HW]
            lr[1, (k + n) * 4:(k + n) * 4 + 4, :] = new[OY - HW:OY]
    for q in range(NQ):
        turned = oc[4 * q:4 * q + 4, 0].reshape(BLK, BLK).T
        ls[0, q * 8:q * 8 + HW, :] = turned[0:HW]
        ls[1, q * 8:q * 8 + HW, :] = turned[BLK - HW:BLK]
    for side in range(2):
        turned = lr[side].T
        lc[2 * side, 0:HW, :] = turned[0:HW]
        lc[2 * side + 1, 0:HW, :] = turned[BLK - HW:BLK]
    late = halo(LATE, lr, lc, ls, lr_in, lc_in, ls_in, 4 * K)
    for copy in late:
        copy.start()

    acc[...] = jnp.zeros_like(acc)

    def return_group(t, carry):
        t = (t + 8) % 9
        g = (t // 2) * (1 - t % 2) + (8 - t // 2) * (t % 2)

        @pl.when(g != 4)
        def _():
            message(SURFACE, g, sbuf.at[g], sin.at[g], -1).wait_recv()

        parts = []
        for s in range(CAP):
            e = g * CAP + s
            hi, lo = split2(wbuf[jnp.maximum(inter[2, e], 0)])
            ahi, alo = split2(sin[g, pl.ds(s, K, stride=CAP), :])
            wets = jnp.broadcast_to(sin[g, pl.ds(K * CAP + s, 1), :], (K, BLK)).astype(BF16)
            lhs = jnp.concatenate([ahi, alo, wets], 0)
            first = dot(lhs, hi)
            second = dot(lhs, lo)
            parts.append((
                first[0:K] + first[K:2 * K] + second[0:K],
                first[2 * K:2 * K + 8] + second[2 * K:2 * K + 8],
            ))
        for b in range(ACB):
            tracers, wets = acc[b, 0:K, :], acc[b, K:K + 8, :]
            for s in range(CAP):
                e = g * CAP + s
                here = jnp.where((inter[0, e] == b) & (inter[1, e] >= 0), 1.0, 0.0).astype(F32)
                tracers = tracers + here * parts[s][0]
                wets = wets + here * parts[s][1]
            acc[b, 0:K, :] = tracers
            acc[b, K:K + 8, :] = wets
        return carry

    lax.fori_loop(0, 9, return_group, 0)
    for b in range(ACB):
        old = abuf[:, 0, b * BLK:(b + 1) * BLK]
        bottom[pl.ds(b, K, stride=ACB), :] = old + air_uptake * (
            acc[b, 0:K, :] - acc[b, K:K + 1, :] * old
        )

    for copy in requests:
        copy.wait_send()
    for copy in early:
        copy.wait()
    for copy in late:
        copy.wait()
    for g in NEIGHBOURS:
        message(CONTRIB, g, cbuf.at[g], cin.at[g]).wait_send()
        message(SURFACE, g, sbuf.at[g], sin.at[g], -1).wait_send()


def exchange(inter, atm, mix, oc, vel, mask, weights):
    vmem = pl.BlockSpec(memory_space=pltpu.VMEM)
    hbm = pl.BlockSpec(memory_space=pltpu.HBM)
    shapes = [
        (K, LA, ACB * BLK), (ACB, LA, BLK), (K * ACB, BLK), (K, OL, OY, BLK), (3, OY, BLK),
        (2, EARLY_ROWS, BLK), (4, 8, BLK), (2, EARLY_STRIP, BLK),
        (2, 4 * K, BLK), (4, 8, BLK), (2, 8 * NQ, BLK),
    ]
    return pl.pallas_call(
        exchange_kernel,
        out_shape=[jax.ShapeDtypeStruct(s, F32) for s in shapes],
        in_specs=[hbm] * 7,
        out_specs=[vmem] * len(shapes),
        scratch_shapes=[
            pltpu.SMEM((3, SLOTS), jnp.int32),
            pltpu.VMEM((WSL, BLK, BLK), F32),
            pltpu.VMEM((K, 8, ACB * BLK), F32),
            pltpu.VMEM((K, LA, ACB * BLK), F32),
            pltpu.VMEM((ACB, LA, LA), F32),
            pltpu.VMEM((OY, BLK), jnp.int32),
            pltpu.VMEM((ACB, LA, 2 * BLK), BF16),
            pltpu.VMEM((ACB, 2 * K, BLK), BF16),
            pltpu.VMEM((9, CAP, BLK), jnp.int32),
            pltpu.VMEM((9, CAP, BLK), jnp.int32),
            pltpu.VMEM((9, K * CAP, BLK), F32),
            pltpu.VMEM((9, K * CAP, BLK), F32),
            pltpu.VMEM((9, (K + 1) * CAP, BLK), F32),
            pltpu.VMEM((9, (K + 1) * CAP, BLK), F32),
            pltpu.VMEM((ACB, K + 8, BLK), F32),
            pltpu.VMEM((2, 2 * BLK, BLK), F32),
            pltpu.VMEM((4, 8, BLK), F32),
            pltpu.VMEM((2, EARLY_STRIP, BLK), F32),
            pltpu.VMEM((2, BLK, BLK), F32),
            pltpu.VMEM((4, 8, BLK), F32),
            pltpu.VMEM((2, 8 * NQ, BLK), F32),
            pltpu.SemaphoreType.DMA((8,)),
            pltpu.SemaphoreType.DMA((8,)),
            pltpu.SemaphoreType.DMA((6,)),
            pltpu.SemaphoreType.DMA((5, 9)),
            pltpu.SemaphoreType.DMA((5, 9)),
        ],
        compiler_params=pltpu.CompilerParams(
            collective_id=0, has_side_effects=True, vmem_limit_bytes=30 * 2**20
        ),
        name="exchange",
    )(*(
        pltpu.with_memory_space_constraint(x, pltpu.HBM)
        for x in (inter, atm, mix, oc, vel, mask, weights)
    ))


def step_kernel(
    mixed, first_column, bottom, oc, own, er, ec, es, lr, lc, ls,
    atm_out, oc_out, coef, xs, ct,
):
    q = pl.program_id(0)

    def spread(east, west):
        gap = jnp.zeros((BLK - 2 * HW, BLK), F32)
        return jnp.concatenate([east, gap, west], 0).T

    @pl.when(q == 0)
    def _():
        for side in range(2):
            for blk in range(2):
                ct[side, blk * BLK:(blk + 1) * BLK, :] = spread(
                    ec[2 * side, blk * HW:(blk + 1) * HW, :],
                    ec[2 * side + 1, blk * HW:(blk + 1) * HW, :],
                )
            ct[side, 2 * BLK:3 * BLK, :] = spread(lc[2 * side, 0:HW, :], lc[2 * side + 1, 0:HW, :])
        ends = spread(es[0, 12:16, :], es[1, 12:16, :])
        fields = []
        for n in range(3):
            row = NQ * 48 + n * 4
            left = jnp.concatenate([own[n], er[0, row:row + HW, :], er[1, row:row + HW, :]], 0)
            right = jnp.concatenate(
                [ends[n * OY:(n + 1) * OY], ct[0, row:row + HW, :], ct[1, row:row + HW, :]], 0
            )
            fields.append(jnp.concatenate([left, right], 1))
        u, v, wet = fields
        coef[0] = wet * (mix_horizontal - 0.5 * u)
        coef[1] = wet * (mix_horizontal + 0.5 * u)
        coef[2] = wet * (mix_horizontal - 0.5 * v)
        coef[3] = wet * (mix_horizontal + 0.5 * v)
        coef[4] = wet * mix_vertical
        coef[5] = wet * (1.0 - 4.0 * mix_horizontal - 2.0 * mix_vertical)
        coef[6] = wet

    for lev in range(OL):
        if lev == 0:
            base = pl.multiple_of(q * 16, 16)
            north, south = lr[0, pl.ds(base, 16), :], lr[1, pl.ds(base, 16), :]
            corner = pl.multiple_of(2 * BLK + q * 16, 16)
            group = pl.multiple_of(q * 8, 8)
            ends = spread(ls[0, pl.ds(group, 8), :][0:HW], ls[1, pl.ds(group, 8), :][0:HW])
        else:
            base = pl.multiple_of(q * 48 + (lev - 1) * 16, 16)
            north, south = er[0, pl.ds(base, 16), :], er[1, pl.ds(base, 16), :]
            corner = base
            group = pl.multiple_of(q * 16, 16)
            piece = slice((lev - 1) * HW, lev * HW)
            ends = spread(es[0, pl.ds(group, 16), :][piece], es[1, pl.ds(group, 16), :][piece])
        north_ends, south_ends = ct[0, pl.ds(corner, 16), :], ct[1, pl.ds(corner, 16), :]
        for p in range(4):
            part = slice(p * 4, p * 4 + 4)
            xs[p, lev, 0:OY, 0:BLK] = oc[4 * q + p, lev]
            xs[p, lev, OY:OY + HW, 0:BLK] = north[part]
            xs[p, lev, OY + HW:EXT_ROWS, 0:BLK] = south[part]
            xs[p, lev, 0:OY, BLK:EXT_COLS] = ends[p * OY:(p + 1) * OY]
            xs[p, lev, OY:OY + HW, BLK:EXT_COLS] = north_ends[part]
            xs[p, lev, OY + HW:EXT_ROWS, BLK:EXT_COLS] = south_ends[part]

    def ocean(p, carry):
        levels = [xs[p, lev] * coef[6] for lev in range(OL)]
        for _ in range(NSUB):
            new = []
            for lev in range(OL):
                x = levels[lev]
                above, below = levels[max(lev - 1, 0)], levels[min(lev + 1, OL - 1)]
                new.append(
                    coef[0] * pltpu.roll(x, EXT_COLS - 1, 1)
                    + coef[1] * pltpu.roll(x, 1, 1)
                    + coef[2] * pltpu.roll(x, EXT_ROWS - 1, 0)
                    + coef[3] * pltpu.roll(x, 1, 0)
                    + coef[4] * (above + below)
                    + coef[5] * x
                )
            levels = new
        for lev in range(OL):
            oc_out[p, lev] = levels[lev][0:OY, 0:BLK]
        return carry

    lax.fori_loop(0, 4, ocean, 0)

    for p in range(4):
        k = 4 * q + p
        surface = bottom[pl.ds(pl.multiple_of(k * ACB, ACB), ACB), :]
        for b in range(ACB):
            cols = slice(b * BLK, (b + 1) * BLK)
            atm_out[p, :, cols] = mixed[k, :, cols] + first_column[b] * surface[b:b + 1]


def local_step(arrays):
    vmem = pl.BlockSpec(memory_space=pltpu.VMEM)
    return pl.pallas_call(
        step_kernel,
        grid=(NQ,),
        out_shape=[
            jax.ShapeDtypeStruct((K, LA, ACB * BLK), F32),
            jax.ShapeDtypeStruct((K, OL, OY, BLK), F32),
        ],
        in_specs=[vmem] * len(arrays),
        out_specs=[
            pl.BlockSpec((4, LA, ACB * BLK), lambda q: (q, 0, 0)),
            pl.BlockSpec((4, OL, OY, BLK), lambda q: (q, 0, 0, 0)),
        ],
        scratch_shapes=[
            pltpu.VMEM((7, EXT_ROWS, EXT_COLS), F32),
            pltpu.VMEM((4, OL, EXT_ROWS, EXT_COLS), F32),
            pltpu.VMEM((2, 3 * BLK, BLK), F32),
        ],
        compiler_params=pltpu.CompilerParams(vmem_limit_bytes=20 * 2**20),
        name="step",
    )(*arrays)


def body(atm, mix, oc, vel, mask, inter, weights):
    return tuple(local_step(exchange(inter, atm, mix, oc, vel, mask, weights)))


def solution(mesh):
    in_specs = (
        P(None, None, ("gx", "gy")),
        P(("gx", "gy"), None, None),
        P(None, None, "gy", "gx"),
        P(None, "gy", "gx"),
        P("gy", "gx"),
        P(None, ("gx", "gy")),
        P(("gx", "gy"), None, None),
    )
    out_specs = (P(None, None, ("gx", "gy")), P(None, None, "gy", "gx"))
    return jax.shard_map(body, mesh=mesh, in_specs=in_specs, out_specs=out_specs, check_vma=False)
```

```python
import functools

import jax
import jax.numpy as jnp
from jax import lax
from jax.experimental import pallas as pl
from jax.experimental.pallas import tpu as pltpu
from jax.sharding import PartitionSpec as P

K = 16
LA = 72
OL = 4
OY = 32
BLK = 128
ACB = 8
CAP = 8
WSL = 64
NSUB = 4
SLOTS = 9 * CAP
HW = NSUB
LANES = OY + 2 * HW
TRIPLES = 6
EARLY_GROUPS = TRIPLES * (OL - 1)
COLS = BLK + 2 * HW
PADDED = COLS + 16

ocean_uptake = 0.5
air_uptake = 0.5
mix_horizontal = 0.15
mix_vertical = 0.2

F32 = jnp.float32
BF16 = jnp.bfloat16
MESH = pl.DeviceIdType.MESH
NEIGHBOURS = (0, 8, 1, 7, 2, 6, 3, 5)
REQUEST, CONTRIB, SURFACE, EARLY, LATE = range(5)
NQ = 4
EARLY_ROWS = NQ * 48 + 16
EARLY_STRIP = 80
LATE_STRIP = 24


def split2(x):
    hi = x.astype(BF16)
    return hi, (x - hi.astype(F32)).astype(BF16)


def split3(x):
    hi = x.astype(BF16)
    rest = x - hi.astype(F32)
    mid = rest.astype(BF16)
    return hi, mid, (rest - mid.astype(F32)).astype(BF16)


def dot(a, b):
    return jnp.dot(a, b, preferred_element_type=F32)


def dot_nt(a, b):
    return lax.dot_general(a, b, (((1,), (1,)), ((), ())), preferred_element_type=F32)


def turned(tiles):
    gap = jnp.zeros((2 * HW, BLK), F32)
    rows = []
    for tile in tiles:
        rows += [tile, gap]
    full = jnp.concatenate(rows, 0)
    if full.shape[0] < BLK:
        full = jnp.concatenate([full, jnp.zeros((BLK - full.shape[0], BLK), F32)], 0)
    return full.T


def cut_edges(groups, strips, ends, lane):
    blocks = {}
    for n, full in groups:
        strips[0, n * HW:(n + 1) * HW, :] = full[0:HW]
        strips[1, n * HW:(n + 1) * HW, :] = full[BLK - HW:BLK]
        edge = jnp.concatenate([full[0:HW], full[BLK - HW:BLK]], 0)
        here = (lane % LANES) // HW == n % 10
        low = pltpu.roll(edge, (n % 10) * HW, 1)
        high = pltpu.roll(edge, ((n % 10) * HW - (OY - HW)) % BLK, 1)
        old = blocks.get(n // 10, (jnp.zeros((8, BLK), F32),) * 2)
        blocks[n // 10] = (jnp.where(here, low, old[0]), jnp.where(here, high, old[1]))
    for b in range(2):
        low, high = blocks.get(b, (jnp.zeros((8, BLK), F32),) * 2)
        rows = slice(b * HW, (b + 1) * HW)
        ends[0, rows, :] = low[0:HW]
        ends[1, rows, :] = low[HW:8]
        ends[2, rows, :] = high[0:HW]
        ends[3, rows, :] = high[HW:8]


def exchange_kernel(
    inter_hbm, atm_hbm, mix_hbm, oc_hbm, vel_hbm, mask_hbm, w_hbm,
    mixed, first_column, bottom, oc, fields, er_in, ec_in, es_in, lr_in, lc_in, ls_in,
    inter, wbuf, abuf, xbuf, mbuf, maskbuf, stacked, ast, req, reqs, cbuf, cin, sbuf, sin, acc,
    er, ec, es, lr, lc, ls,
    wsem, xsem, lsem, ssem, rsem,
):
    nx, ny = lax.axis_size("gx"), lax.axis_size("gy")
    i, j = lax.axis_index("gx"), lax.axis_index("gy")

    def device(g, sign):
        dy, dx = g // 3 - 1, g % 3 - 1
        return ((i + sign * dx + nx) % nx, (j + sign * dy + ny) % ny)

    def message(kind, g, src, dst, sign=1):
        return pltpu.make_async_remote_copy(
            src_ref=src, dst_ref=dst, send_sem=ssem.at[kind, g], recv_sem=rsem.at[kind, g],
            device_id=device(g, sign), device_id_type=MESH,
        )

    barrier = pltpu.get_barrier_semaphore()
    for g in NEIGHBOURS:
        pl.semaphore_signal(barrier, inc=1, device_id=device(g, 1), device_id_type=MESH)

    chunk = WSL // 8
    small = [
        pltpu.make_async_copy(src, dst, lsem.at[n])
        for n, (src, dst) in enumerate((
            (oc_hbm, oc), (vel_hbm, fields.at[pl.ds(0, 2)]), (mask_hbm, maskbuf),
            (atm_hbm.at[:, pl.ds(0, 8), :], abuf), (mix_hbm, mbuf), (inter_hbm, inter),
        ))
    ]
    loads = [
        pltpu.make_async_copy(
            w_hbm.at[pl.ds(c * chunk, chunk)], wbuf.at[pl.ds(c * chunk, chunk)], wsem.at[c]
        )
        for c in range(8)
    ]
    columns = [
        pltpu.make_async_copy(atm_hbm.at[pl.ds(2 * c, 2)], xbuf.at[pl.ds(2 * c, 2)], xsem.at[c])
        for c in range(8)
    ]
    for load in small[5:6] + small[0:5] + loads:
        load.start()

    small[5].wait()
    for e in range(SLOTS):
        req[e // CAP, pl.ds(e % CAP, 1), :] = jnp.full((1, BLK), inter[1, e], jnp.int32)
    reqs[4] = req[4]
    for load in small[0:3]:
        load.wait()
    wet = maskbuf[...].astype(F32)
    fields[2] = wet
    vel = fields

    er[:, NQ * 48 + 8:EARLY_ROWS, :] = jnp.zeros((2, 8, BLK), F32)
    es[:, 72:EARLY_STRIP, :] = jnp.zeros((2, 8, BLK), F32)
    lane = lax.broadcasted_iota(jnp.int32, (8, BLK), 1)
    for q in range(NQ):
        for lev in range(1, OL):
            for p in range(4):
                row = q * 48 + (lev - 1) * 16 + p * 4
                er[0, row:row + HW, :] = oc[4 * q + p, lev, 0:HW, :]
                er[1, row:row + HW, :] = oc[4 * q + p, lev, OY - HW:OY, :]
    for n in range(3):
        row = NQ * 48 + n * 4
        field = vel[n] if n < 2 else wet
        er[0, row:row + HW, :] = field[0:HW]
        er[1, row:row + HW, :] = field[OY - HW:OY]
    groups = [
        (t * 3 + lev - 1, turned([oc[k, lev] for k in range(3 * t, min(3 * t + 3, K))]))
        for t in range(TRIPLES) for lev in range(1, OL)
    ]
    cut_edges(groups + [(EARLY_GROUPS, turned([vel[0], vel[1], wet]))], es, ec, lane)

    pl.semaphore_wait(barrier, len(NEIGHBOURS))

    requests = [message(REQUEST, g, req.at[g], reqs.at[g]) for g in NEIGHBOURS]
    for copy in requests:
        copy.start()

    sides = {1: 0, 7: 1}
    ends = {3: 0, 5: 1}
    corners = {0: 0, 2: 1, 6: 2, 8: 3}

    def halo(kind, rows, corner, strip, rows_in, corner_in, strip_in, count):
        copies = []
        for g in NEIGHBOURS:
            if g in sides:
                n = sides[g]
                copies.append(message(kind, g, rows.at[n, pl.ds(0, count)], rows_in.at[n]))
            elif g in ends:
                n = ends[g]
                copies.append(message(kind, g, strip.at[n], strip_in.at[n]))
            else:
                n = corners[g]
                copies.append(message(kind, g, corner.at[n], corner_in.at[n]))
        return copies

    early = halo(EARLY, er, ec, es, er_in, ec_in, es_in, EARLY_ROWS)
    for copy in early:
        copy.start()

    small[3].wait()
    for b in range(ACB):
        block = abuf[:, 0, b * BLK:(b + 1) * BLK]
        hi, lo = split2(block)
        ast[b, 0:K, :] = hi
        ast[b, K:2 * K, :] = lo
    for load in loads:
        load.wait()
    for load in columns:
        load.start()

    def contrib_group(t, carry):
        g = (t // 2) * (1 - t % 2) + (8 - t // 2) * (t % 2)
        for s in range(CAP):
            e = g * CAP + s
            hi, lo = split2(wbuf[jnp.maximum(inter[2, e], 0)])
            a = ast[jnp.maximum(inter[0, e], 0)]
            first = dot_nt(a, hi)
            second = dot_nt(a[0:K], lo)
            cbuf[g, pl.ds(s, K, stride=CAP), :] = first[0:K] + first[K:2 * K] + second

        @pl.when(g != 4)
        def _():
            message(CONTRIB, g, cbuf.at[g], cin.at[g]).start()

        return carry

    lax.fori_loop(0, 9, contrib_group, 0)
    cin[4] = cbuf[4]

    for copy in requests:
        copy.wait_recv()
    lanes = lax.broadcasted_iota(jnp.int32, (SLOTS, BLK), 1)
    chosen = (reqs[...].reshape(SLOTS, BLK) == lanes).astype(F32)
    pick = chosen[:, 0:OY].astype(BF16)
    for k in range(0, K, 2):
        pair = jnp.concatenate([oc[k, 0] * wet, oc[k + 1, 0] * wet], 1)
        hi, mid, lo = split3(pair)
        rows = dot(pick, hi) + dot(pick, mid) + dot(pick, lo)
        for g in range(9):
            sbuf[g, k * CAP:(k + 1) * CAP, :] = rows[g * CAP:(g + 1) * CAP, 0:BLK]
            sbuf[g, (k + 1) * CAP:(k + 2) * CAP, :] = rows[g * CAP:(g + 1) * CAP, BLK:2 * BLK]
    rows = dot(pick, wet.astype(BF16))
    for g in range(9):
        sbuf[g, K * CAP:(K + 1) * CAP, :] = rows[g * CAP:(g + 1) * CAP]
    sin[4] = sbuf[4]
    for g in NEIGHBOURS:
        message(SURFACE, g, sbuf.at[g], sin.at[g], -1).start()

    small[4].wait()
    for b in range(ACB):
        m = jnp.concatenate([mbuf[b], jnp.zeros((LA, 2 * BLK - LA), F32)], 1)
        first_column[b] = jnp.broadcast_to(m[:, 0:1], (LA, BLK))
        mh = m.astype(BF16).astype(F32)
        stacked[b] = (mh + pltpu.roll(mh, 80, 1) + pltpu.roll(m - mh, 160, 1)).astype(BF16)
    upper = lax.broadcasted_iota(jnp.int32, (8, BLK), 0) > 0

    for c in range(8):
        columns[c].wait()

    def mixing(c, carry):
        for b in range(ACB):
            cols = slice(b * BLK, (b + 1) * BLK)
            sides = []
            for n in range(2):
                x = jnp.concatenate([
                    jnp.where(upper, xbuf[2 * c + n, 0:8, cols], 0.0),
                    xbuf[2 * c + n, 8:LA, cols],
                    jnp.zeros((8, BLK), F32),
                ], 0)
                hi, lo = split2(x)
                sides.append(jnp.concatenate([hi, lo, hi, jnp.zeros((16, BLK), BF16)], 0))
            out = dot(stacked[b], jnp.concatenate(sides, 1))
            mixed[2 * c, :, cols] = out[:, 0:BLK]
            mixed[2 * c + 1, :, cols] = out[:, BLK:2 * BLK]
        return carry

    lax.fori_loop(0, 8, mixing, 0)

    place = chosen.T[0:OY].astype(BF16)
    for g in NEIGHBOURS:
        message(CONTRIB, g, cbuf.at[g], cin.at[g]).wait_recv()
    for k in range(0, K, 2):
        pair = jnp.concatenate(
            [cin[:, n * CAP:(n + 1) * CAP, :].reshape(SLOTS, BLK) for n in (k, k + 1)], 1
        )
        hi, mid, lo = split3(pair)
        arrived = dot(place, hi) + dot(place, mid) + dot(place, lo)
        for n in range(2):
            old = oc[k + n, 0]
            new = old + ocean_uptake * wet * (arrived[:, n * BLK:(n + 1) * BLK] - old)
            oc[k + n, 0] = new
            lr[0, (k + n) * 4:(k + n) * 4 + 4, :] = new[0:HW]
            lr[1, (k + n) * 4:(k + n) * 4 + 4, :] = new[OY - HW:OY]
    groups = [
        (t, turned([oc[k, 0] for k in range(3 * t, min(3 * t + 3, K))])) for t in range(TRIPLES)
    ]
    cut_edges(groups, ls, lc, lane)
    late = halo(LATE, lr, lc, ls, lr_in, lc_in, ls_in, 4 * K)
    for copy in late:
        copy.start()

    acc[...] = jnp.zeros_like(acc)

    def return_group(t, carry):
        t = (t + 8) % 9
        g = (t // 2) * (1 - t % 2) + (8 - t // 2) * (t % 2)

        @pl.when(g != 4)
        def _():
            message(SURFACE, g, sbuf.at[g], sin.at[g], -1).wait_recv()

        parts = []
        for s in range(CAP):
            e = g * CAP + s
            hi, lo = split2(wbuf[jnp.maximum(inter[2, e], 0)])
            ahi, alo = split2(sin[g, pl.ds(s, K, stride=CAP), :])
            wets = jnp.broadcast_to(sin[g, pl.ds(K * CAP + s, 1), :], (K, BLK)).astype(BF16)
            lhs = jnp.concatenate([ahi, alo, wets], 0)
            first = dot(lhs, hi)
            second = dot(lhs, lo)
            parts.append((
                first[0:K] + first[K:2 * K] + second[0:K],
                first[2 * K:2 * K + 8] + second[2 * K:2 * K + 8],
            ))
        for b in range(ACB):
            tracers, wets = acc[b, 0:K, :], acc[b, K:K + 8, :]
            for s in range(CAP):
                e = g * CAP + s
                here = jnp.where((inter[0, e] == b) & (inter[1, e] >= 0), 1.0, 0.0).astype(F32)
                tracers = tracers + here * parts[s][0]
                wets = wets + here * parts[s][1]
            acc[b, 0:K, :] = tracers
            acc[b, K:K + 8, :] = wets
        return carry

    lax.fori_loop(0, 9, return_group, 0)
    for b in range(ACB):
        old = abuf[:, 0, b * BLK:(b + 1) * BLK]
        bottom[pl.ds(b, K, stride=ACB), :] = old + air_uptake * (
            acc[b, 0:K, :] - acc[b, K:K + 1, :] * old
        )

    for copy in requests:
        copy.wait_send()
    for copy in early:
        copy.wait()
    for copy in late:
        copy.wait()
    for g in NEIGHBOURS:
        message(CONTRIB, g, cbuf.at[g], cin.at[g]).wait_send()
        message(SURFACE, g, sbuf.at[g], sin.at[g], -1).wait_send()


def exchange(inter, atm, mix, oc, vel, mask, weights):
    vmem = pl.BlockSpec(memory_space=pltpu.VMEM)
    hbm = pl.BlockSpec(memory_space=pltpu.HBM)
    shapes = [
        (K, LA, ACB * BLK), (ACB, LA, BLK), (K * ACB, BLK), (K, OL, OY, BLK), (3, OY, BLK),
        (2, EARLY_ROWS, BLK), (4, 8, BLK), (2, EARLY_STRIP, BLK),
        (2, 4 * K, BLK), (4, 8, BLK), (2, LATE_STRIP, BLK),
    ]
    return pl.pallas_call(
        exchange_kernel,
        out_shape=[jax.ShapeDtypeStruct(s, F32) for s in shapes],
        in_specs=[hbm] * 7,
        out_specs=[vmem] * len(shapes),
        scratch_shapes=[
            pltpu.SMEM((3, SLOTS), jnp.int32),
            pltpu.VMEM((WSL, BLK, BLK), F32),
            pltpu.VMEM((K, 8, ACB * BLK), F32),
            pltpu.VMEM((K, LA, ACB * BLK), F32),
            pltpu.VMEM((ACB, LA, LA), F32),
            pltpu.VMEM((OY, BLK), jnp.int32),
            pltpu.VMEM((ACB, LA, 2 * BLK), BF16),
            pltpu.VMEM((ACB, 2 * K, BLK), BF16),
            pltpu.VMEM((9, CAP, BLK), jnp.int32),
            pltpu.VMEM((9, CAP, BLK), jnp.int32),
            pltpu.VMEM((9, K * CAP, BLK), F32),
            pltpu.VMEM((9, K * CAP, BLK), F32),
            pltpu.VMEM((9, (K + 1) * CAP, BLK), F32),
            pltpu.VMEM((9, (K + 1) * CAP, BLK), F32),
            pltpu.VMEM((ACB, K + 8, BLK), F32),
            pltpu.VMEM((2, EARLY_ROWS, BLK), F32),
            pltpu.VMEM((4, 8, BLK), F32),
            pltpu.VMEM((2, EARLY_STRIP, BLK), F32),
            pltpu.VMEM((2, 4 * K, BLK), F32),
            pltpu.VMEM((4, 8, BLK), F32),
            pltpu.VMEM((2, LATE_STRIP, BLK), F32),
            pltpu.SemaphoreType.DMA((8,)),
            pltpu.SemaphoreType.DMA((8,)),
            pltpu.SemaphoreType.DMA((6,)),
            pltpu.SemaphoreType.DMA((5, 9)),
            pltpu.SemaphoreType.DMA((5, 9)),
        ],
        compiler_params=pltpu.CompilerParams(
            collective_id=0, has_side_effects=True, vmem_limit_bytes=30 * 2**20
        ),
        name="exchange",
    )(*(
        pltpu.with_memory_space_constraint(x, pltpu.HBM)
        for x in (inter, atm, mix, oc, vel, mask, weights)
    ))


def step_kernel(
    mixed, first_column, bottom, oc, own, er, ec, es, lr, lc, ls,
    atm_out, oc_out, atm_stage, oc_stage, coef, state, work, asem, osem,
):
    def surface_part(k, carry):
        surface = bottom[pl.ds(pl.multiple_of(k * ACB, ACB), ACB), :]
        for b in range(ACB):
            cols = slice(b * BLK, (b + 1) * BLK)
            atm_stage[k, :, cols] = mixed[k, :, cols] + first_column[b] * surface[b:b + 1]
        pltpu.make_async_copy(atm_stage.at[k], atm_out.at[k], asem.at[k]).start()
        return carry

    lax.fori_loop(0, K, surface_part, 0)

    lane = lax.broadcasted_iota(jnp.int32, (8, BLK), 1)
    shifted = (lane + HW) % BLK
    north = (shifted % LANES >= OY + HW) & (shifted < 3 * LANES)
    south = (shifted % LANES < HW) & (shifted < 3 * LANES)

    def widen(tiles, norths, souths):
        gap = jnp.zeros((HW, BLK), F32)
        rows = []
        for n in range(3):
            n_row = norths[n] if n < len(tiles) else gap
            s_row = souths[n + 1] if n + 1 < len(tiles) else gap
            rows += [tiles[n] if n < len(tiles) else jnp.zeros((OY, BLK), F32), n_row, s_row]
        return jnp.concatenate(rows + [gap, souths[0]], 0).T

    def edges(strips, ends, n):
        rows = slice((n // 10) * HW, (n // 10 + 1) * HW)
        mine = jnp.concatenate(
            [strips[0, n * HW:(n + 1) * HW, :], strips[1, n * HW:(n + 1) * HW, :]], 0
        )
        above = jnp.concatenate([ends[0, rows, :], ends[1, rows, :]], 0)
        below = jnp.concatenate([ends[2, rows, :], ends[3, rows, :]], 0)
        above = pltpu.roll(above, (OY - (n % 10) * HW) % BLK, 1)
        below = pltpu.roll(below, (BLK - HW - (n % 10) * HW) % BLK, 1)
        return jnp.where(north, above, jnp.where(south, below, mine))

    fields = []
    ends = edges(es, ec, EARLY_GROUPS)
    for n in range(3):
        row = NQ * 48 + n * HW
        inner = widen([own[n]] * 3, [er[0, row:row + HW, :]] * 3, [er[1, row:row + HW, :]] * 3)
        parts = [pltpu.roll(ends, ((m - n) * LANES) % BLK, 1) for m in range(3)]
        outer = jnp.where(
            shifted < LANES, parts[0], jnp.where(shifted < 2 * LANES, parts[1], parts[2])
        )
        fields.append(jnp.concatenate([inner, outer], 0))
    u, v, wet = fields
    coef[0] = wet * (mix_horizontal - 0.5 * u)
    coef[1] = wet * (mix_horizontal + 0.5 * u)
    coef[2] = wet * (mix_horizontal - 0.5 * v)
    coef[3] = wet * (mix_horizontal + 0.5 * v)
    coef[4] = wet * mix_vertical
    coef[5] = wet * (1.0 - 4.0 * mix_horizontal - 2.0 * mix_vertical)
    coef[6] = wet

    for t in range(TRIPLES):
        ks = range(3 * t, min(3 * t + 3, K))
        for lev in range(OL):
            if lev == 0:
                halo = [[lr[side, k * HW:(k + 1) * HW, :] for k in ks] for side in range(2)]
                outer = edges(ls, lc, t)
            else:
                rows = [(k // 4) * 48 + (lev - 1) * 16 + (k % 4) * HW for k in ks]
                halo = [[er[side, row:row + HW, :] for row in rows] for side in range(2)]
                outer = edges(es, ec, t * 3 + lev - 1)
            inner = widen([oc[k, lev] for k in ks], *halo) * coef[6, 0:BLK, :]
            outer = outer * coef[6, BLK:COLS, :]
            state[t, lev, 0:8, :] = outer
            state[t, lev, 8:8 + BLK, :] = inner
            state[t, lev, 8 + BLK:8 + COLS, :] = outer
            state[t, lev, 8 + COLS:PADDED, :] = inner[0:8]

    def ocean(t, carry):
        for sub in range(NSUB):
            def source(lev, start):
                if sub == 0:
                    return state[t, lev, start:start + 8, :]
                return work[(sub - 1) % 2, lev, start:start + 8, :]

            for tile in range(COLS // 8):
                start = 8 + tile * 8
                c = [coef[n, tile * 8:tile * 8 + 8, :] for n in range(6)]
                x = [source(lev, start) for lev in range(OL)]
                for lev in range(OL):
                    new = (
                        c[0] * source(lev, start + 1)
                        + c[1] * source(lev, start - 1)
                        + c[2] * pltpu.roll(x[lev], BLK - 1, 1)
                        + c[3] * pltpu.roll(x[lev], 1, 1)
                        + c[4] * (x[max(lev - 1, 0)] + x[min(lev + 1, OL - 1)])
                        + c[5] * x[lev]
                    )
                    work[sub % 2, lev, start:start + 8, :] = new
                    if tile == 0:
                        work[sub % 2, lev, 8 + COLS:PADDED, :] = new
                    if tile == COLS // 8 - 1:
                        work[sub % 2, lev, 0:8, :] = new
        for lev in range(OL):
            out = work[(NSUB - 1) % 2, lev, 8:8 + BLK, :].T
            for n in range(3):
                oc_stage[3 * t + n, lev] = out[n * LANES:n * LANES + OY]

        @pl.when(t < TRIPLES - 1)
        def _():
            pltpu.make_async_copy(
                oc_stage.at[pl.ds(3 * t, 3)], oc_out.at[pl.ds(3 * t, 3)], osem.at[t]
            ).start()

        return carry

    lax.fori_loop(0, TRIPLES, ocean, 0)
    last = pltpu.make_async_copy(
        oc_stage.at[pl.ds(K - 1, 1)], oc_out.at[pl.ds(K - 1, 1)], osem.at[TRIPLES - 1]
    )
    last.start()
    for k in range(K):
        pltpu.make_async_copy(atm_stage.at[k], atm_out.at[k], asem.at[k]).wait()
    for t in range(TRIPLES - 1):
        pltpu.make_async_copy(
            oc_stage.at[pl.ds(3 * t, 3)], oc_out.at[pl.ds(3 * t, 3)], osem.at[t]
        ).wait()
    last.wait()


def local_step(arrays):
    vmem = pl.BlockSpec(memory_space=pltpu.VMEM)
    hbm = pl.BlockSpec(memory_space=pltpu.HBM)
    return pl.pallas_call(
        step_kernel,
        out_shape=[
            jax.ShapeDtypeStruct((K, LA, ACB * BLK), F32),
            jax.ShapeDtypeStruct((K, OL, OY, BLK), F32),
        ],
        in_specs=[vmem] * len(arrays),
        out_specs=[hbm, hbm],
        scratch_shapes=[
            pltpu.VMEM((K, LA, ACB * BLK), F32),
            pltpu.VMEM((3 * TRIPLES, OL, OY, BLK), F32),
            pltpu.VMEM((7, COLS, BLK), F32),
            pltpu.VMEM((TRIPLES, OL, PADDED, BLK), F32),
            pltpu.VMEM((2, OL, PADDED, BLK), F32),
            pltpu.SemaphoreType.DMA((K,)),
            pltpu.SemaphoreType.DMA((TRIPLES,)),
        ],
        compiler_params=pltpu.CompilerParams(vmem_limit_bytes=20 * 2**20),
        name="step",
    )(*arrays)


def body(atm, mix, oc, vel, mask, inter, weights):
    return tuple(local_step(exchange(inter, atm, mix, oc, vel, mask, weights)))


def solution(mesh):
    in_specs = (
        P(None, None, ("gx", "gy")),
        P(("gx", "gy"), None, None),
        P(None, None, "gy", "gx"),
        P(None, "gy", "gx"),
        P("gy", "gx"),
        P(None, ("gx", "gy")),
        P(("gx", "gy"), None, None),
    )
    out_specs = (P(None, None, ("gx", "gy")), P(None, None, "gy", "gx"))
    return jax.shard_map(body, mesh=mesh, in_specs=in_specs, out_specs=out_specs, check_vma=False)
```

```python
import functools

import jax
import jax.numpy as jnp
from jax import lax
from jax.experimental import pallas as pl
from jax.experimental.pallas import tpu as pltpu
from jax.sharding import PartitionSpec as P

K = 16
LA = 72
OL = 4
OY = 32
BLK = 128
ACB = 8
CAP = 8
WSL = 64
NSUB = 4
SLOTS = 9 * CAP
HW = NSUB
LANES = OY + 2 * HW
TRIPLES = 6
EARLY_GROUPS = TRIPLES * (OL - 1)
COLS = BLK + 2 * HW
PADDED = COLS + 16

ocean_uptake = 0.5
air_uptake = 0.5
mix_horizontal = 0.15
mix_vertical = 0.2

F32 = jnp.float32
BF16 = jnp.bfloat16
MESH = pl.DeviceIdType.MESH
NEIGHBOURS = (0, 8, 1, 7, 2, 6, 3, 5)
REQUEST, CONTRIB, SURFACE, EARLY, LATE = range(5)
NQ = 4
EARLY_ROWS = NQ * 48 + 16
EARLY_STRIP = 96
LATE_STRIP = 24


def split2(x):
    hi = x.astype(BF16)
    return hi, (x - hi.astype(F32)).astype(BF16)


def split3(x):
    hi = x.astype(BF16)
    rest = x - hi.astype(F32)
    mid = rest.astype(BF16)
    return hi, mid, (rest - mid.astype(F32)).astype(BF16)


def dot(a, b):
    return jnp.dot(a, b, preferred_element_type=F32)


def dot_nt(a, b):
    return lax.dot_general(a, b, (((1,), (1,)), ((), ())), preferred_element_type=F32)


def turned(tiles):
    gap = jnp.zeros((2 * HW, BLK), F32)
    rows = []
    for tile in tiles:
        rows += [tile, gap]
    full = jnp.concatenate(rows, 0)
    if full.shape[0] < BLK:
        full = jnp.concatenate([full, jnp.zeros((BLK - full.shape[0], BLK), F32)], 0)
    return full.T


def cut_edges(groups, strips, ends, lane):
    blocks = {}
    for n, full in groups:
        strips[0, n * HW:(n + 1) * HW, :] = full[0:HW]
        strips[1, n * HW:(n + 1) * HW, :] = full[BLK - HW:BLK]
        edge = jnp.concatenate([full[0:HW], full[BLK - HW:BLK]], 0)
        here = (lane % LANES) // HW == n % 10
        low = pltpu.roll(edge, (n % 10) * HW, 1)
        high = pltpu.roll(edge, ((n % 10) * HW - (OY - HW)) % BLK, 1)
        old = blocks.get(n // 10, (jnp.zeros((8, BLK), F32),) * 2)
        blocks[n // 10] = (jnp.where(here, low, old[0]), jnp.where(here, high, old[1]))
    for b in range(2):
        low, high = blocks.get(b, (jnp.zeros((8, BLK), F32),) * 2)
        rows = slice(b * HW, (b + 1) * HW)
        ends[0, rows, :] = low[0:HW]
        ends[1, rows, :] = low[HW:8]
        ends[2, rows, :] = high[0:HW]
        ends[3, rows, :] = high[HW:8]


def widen(tiles, norths, souths):
    gap = jnp.zeros((HW, BLK), F32)
    rows = []
    for n in range(3):
        n_row = norths[n] if n < len(tiles) else gap
        s_row = souths[n + 1] if n + 1 < len(tiles) else gap
        rows += [tiles[n] if n < len(tiles) else jnp.zeros((OY, BLK), F32), n_row, s_row]
    return jnp.concatenate(rows + [gap, souths[0]], 0).T


def outer_columns(strips, ends, n, lane):
    shifted = (lane + HW) % BLK
    north = (shifted % LANES >= OY + HW) & (shifted < 3 * LANES)
    south = (shifted % LANES < HW) & (shifted < 3 * LANES)
    rows = slice((n // 10) * HW, (n // 10 + 1) * HW)
    mine = jnp.concatenate(
        [strips[0, n * HW:(n + 1) * HW, :], strips[1, n * HW:(n + 1) * HW, :]], 0
    )
    above = jnp.concatenate([ends[0, rows, :], ends[1, rows, :]], 0)
    below = jnp.concatenate([ends[2, rows, :], ends[3, rows, :]], 0)
    above = pltpu.roll(above, (OY - (n % 10) * HW) % BLK, 1)
    below = pltpu.roll(below, (BLK - HW - (n % 10) * HW) % BLK, 1)
    return jnp.where(north, above, jnp.where(south, below, mine))


def store_tile(state, coef, t, lev, inner, outer):
    inner = inner * coef[6, 0:BLK, :]
    outer = outer * coef[6, BLK:COLS, :]
    state[t, lev, 0:8, :] = outer
    state[t, lev, 8:8 + BLK, :] = inner
    state[t, lev, 8 + BLK:8 + COLS, :] = outer
    state[t, lev, 8 + COLS:PADDED, :] = inner[0:8]


def set_coefficients(coef, own, er, ends, lane):
    shifted = (lane + HW) % BLK
    fields = []
    for n in range(3):
        row = NQ * 48 + n * HW
        inner = widen([own[n]] * 3, [er[0, row:row + HW, :]] * 3, [er[1, row:row + HW, :]] * 3)
        parts = [pltpu.roll(ends, ((m - n) * LANES) % BLK, 1) for m in range(3)]
        outer = jnp.where(
            shifted < LANES, parts[0], jnp.where(shifted < 2 * LANES, parts[1], parts[2])
        )
        fields.append(jnp.concatenate([inner, outer], 0))
    u, v, wet = fields
    coef[0] = wet * (mix_horizontal - 0.5 * u)
    coef[1] = wet * (mix_horizontal + 0.5 * u)
    coef[2] = wet * (mix_horizontal - 0.5 * v)
    coef[3] = wet * (mix_horizontal + 0.5 * v)
    coef[4] = wet * mix_vertical
    coef[5] = wet * (1.0 - 4.0 * mix_horizontal - 2.0 * mix_vertical)
    coef[6] = wet


def exchange_kernel(
    inter_hbm, atm_hbm, mix_hbm, oc_hbm, vel_hbm, mask_hbm, w_hbm,
    mixed, first_column, bottom, coef, state,
    inter, oc, fields, wbuf, abuf, xbuf, mbuf, maskbuf, stacked, ast,
    req, reqs, cbuf, cin, sbuf, sin, acc,
    er, ec, es, lr, lc, ls, er_in, ec_in, es_in, lr_in, lc_in, ls_in,
    wsem, xsem, lsem, ssem, rsem, surf_sem,
):
    nx, ny = lax.axis_size("gx"), lax.axis_size("gy")
    i, j = lax.axis_index("gx"), lax.axis_index("gy")

    def device(g, sign):
        dy, dx = g // 3 - 1, g % 3 - 1
        return ((i + sign * dx + nx) % nx, (j + sign * dy + ny) % ny)

    def message(kind, g, src, dst, sign=1):
        return pltpu.make_async_remote_copy(
            src_ref=src, dst_ref=dst, send_sem=ssem.at[kind],
            recv_sem=surf_sem.at[g] if kind == SURFACE else rsem.at[kind],
            device_id=device(g, sign), device_id_type=MESH,
        )

    def all_of(kind, sem, span):
        pltpu.make_async_copy(span, span, sem.at[kind]).wait()

    spans = {
        REQUEST: req.at[pl.ds(0, 8)], CONTRIB: cbuf.at[pl.ds(0, 8)], SURFACE: sbuf.at[pl.ds(0, 8)],
        EARLY: wbuf.at[pl.ds(0, 5)], LATE: er.at[0],
    }

    barrier = pltpu.get_barrier_semaphore()
    for g in NEIGHBOURS:
        pl.semaphore_signal(barrier, inc=1, device_id=device(g, 1), device_id_type=MESH)

    small = [
        pltpu.make_async_copy(src, dst, lsem.at[n])
        for n, (src, dst) in enumerate((
            (oc_hbm, oc), (vel_hbm, fields.at[pl.ds(0, 2)]), (mask_hbm, maskbuf),
            (atm_hbm.at[:, pl.ds(0, 8), :], abuf), (mix_hbm, mbuf), (inter_hbm, inter),
        ))
    ]
    weights = pltpu.make_async_copy(w_hbm, wbuf, wsem)
    columns = pltpu.make_async_copy(atm_hbm, xbuf, xsem)
    small[5].start()
    small[3].start()
    weights.start()

    small[5].wait()
    for e in range(SLOTS):
        req[e // CAP, pl.ds(e % CAP, 1), :] = jnp.full((1, BLK), inter[1, e], jnp.int32)
    reqs[4] = req[4]

    small[3].wait()
    for b in range(ACB):
        block = abuf[:, 0, b * BLK:(b + 1) * BLK]
        hi, lo = split2(block)
        ast[b, 0:K, :] = hi
        ast[b, K:2 * K, :] = lo
    for load in small[0:3] + small[4:5]:
        load.start()
    weights.wait()
    columns.start()

    def contrib_rows(g):
        for s in range(CAP):
            e = g * CAP + s
            hi, lo = split2(wbuf[jnp.maximum(inter[2, e], 0)])
            a = ast[jnp.maximum(inter[0, e], 0)]
            first = dot_nt(a, hi)
            second = dot_nt(a[0:K], lo)
            cbuf[g, pl.ds(s, K, stride=CAP), :] = first[0:K] + first[K:2 * K] + second

    contrib_rows(NEIGHBOURS[0])
    pl.semaphore_wait(barrier, len(NEIGHBOURS))

    requests = [message(REQUEST, g, req.at[g], reqs.at[g]) for g in NEIGHBOURS]
    for copy in requests:
        copy.start()

    message(CONTRIB, NEIGHBOURS[0], cbuf.at[NEIGHBOURS[0]], cin.at[NEIGHBOURS[0]]).start()

    def contrib_group(t, carry):
        g = (t // 2) * (1 - t % 2) + (8 - t // 2) * (t % 2)
        contrib_rows(g)

        @pl.when(g != 4)
        def _():
            message(CONTRIB, g, cbuf.at[g], cin.at[g]).start()

        return carry

    lax.fori_loop(1, 9, contrib_group, 0)
    cin[4] = cbuf[4]

    for load in small[0:3]:
        load.wait()
    wet = maskbuf[...].astype(F32)
    fields[2] = wet
    vel = fields

    er[:, NQ * 48 + 8:EARLY_ROWS, :] = jnp.zeros((2, 8, BLK), F32)
    es[:, 72:EARLY_STRIP, :] = jnp.zeros((2, EARLY_STRIP - 72, BLK), F32)
    lane = lax.broadcasted_iota(jnp.int32, (8, BLK), 1)
    for q in range(NQ):
        for lev in range(1, OL):
            for p in range(4):
                row = q * 48 + (lev - 1) * 16 + p * 4
                er[0, row:row + HW, :] = oc[4 * q + p, lev, 0:HW, :]
                er[1, row:row + HW, :] = oc[4 * q + p, lev, OY - HW:OY, :]
    for n in range(3):
        row = NQ * 48 + n * 4
        field = vel[n] if n < 2 else wet
        er[0, row:row + HW, :] = field[0:HW]
        er[1, row:row + HW, :] = field[OY - HW:OY]
    groups = [
        (t * 3 + lev - 1, turned([oc[k, lev] for k in range(3 * t, min(3 * t + 3, K))]))
        for t in range(TRIPLES) for lev in range(1, OL)
    ]
    cut_edges(groups + [(EARLY_GROUPS, turned([vel[0], vel[1], wet]))], es, ec, lane)

    sides = {1: 0, 7: 1}
    ends = {3: 0, 5: 1}
    corners = {0: 0, 2: 1, 6: 2, 8: 3}

    def halo(kind, rows, corner, strip, rows_in, corner_in, strip_in, count):
        copies = []
        for g in NEIGHBOURS:
            if g in sides:
                n = sides[g]
                copies.append(message(kind, g, rows.at[n, pl.ds(0, count)], rows_in.at[n]))
            elif g in ends:
                n = ends[g]
                copies.append(message(kind, g, strip.at[n], strip_in.at[n]))
            else:
                n = corners[g]
                copies.append(message(kind, g, corner.at[n], corner_in.at[n]))
        return copies

    early = halo(EARLY, er, ec, es, er_in, ec_in, es_in, EARLY_ROWS)
    for copy in early:
        copy.start()

    all_of(REQUEST, rsem, spans[REQUEST])
    lanes = lax.broadcasted_iota(jnp.int32, (SLOTS, BLK), 1)
    chosen = (reqs[...].reshape(SLOTS, BLK) == lanes).astype(F32)
    pick = chosen[:, 0:OY].astype(BF16)
    for k in range(0, K, 2):
        pair = jnp.concatenate([oc[k, 0] * wet, oc[k + 1, 0] * wet], 1)
        hi, mid, lo = split3(pair)
        rows = dot(pick, hi) + dot(pick, mid) + dot(pick, lo)
        for g in range(9):
            sbuf[g, k * CAP:(k + 1) * CAP, :] = rows[g * CAP:(g + 1) * CAP, 0:BLK]
            sbuf[g, (k + 1) * CAP:(k + 2) * CAP, :] = rows[g * CAP:(g + 1) * CAP, BLK:2 * BLK]
    rows = dot(pick, wet.astype(BF16))
    for g in range(9):
        sbuf[g, K * CAP:(K + 1) * CAP, :] = rows[g * CAP:(g + 1) * CAP]
    sin[4] = sbuf[4]
    for g in NEIGHBOURS:
        message(SURFACE, g, sbuf.at[g], sin.at[g], -1).start()

    small[4].wait()
    for b in range(ACB):
        m = jnp.concatenate([mbuf[b], jnp.zeros((LA, 2 * BLK - LA), F32)], 1)
        first_column[b] = jnp.broadcast_to(m[:, 0:1], (LA, BLK))
        mh = m.astype(BF16).astype(F32)
        stacked[b] = (mh + pltpu.roll(mh, 80, 1) + pltpu.roll(m - mh, 160, 1)).astype(BF16)
    upper = lax.broadcasted_iota(jnp.int32, (8, BLK), 0) > 0

    columns.wait()

    def mixing(c, carry):
        for b in range(ACB):
            cols = slice(b * BLK, (b + 1) * BLK)
            sides = []
            for n in range(2):
                x = jnp.concatenate([
                    jnp.where(upper, xbuf[2 * c + n, 0:8, cols], 0.0),
                    xbuf[2 * c + n, 8:LA, cols],
                    jnp.zeros((8, BLK), F32),
                ], 0)
                hi, lo = split2(x)
                sides.append(jnp.concatenate([hi, lo, hi, jnp.zeros((16, BLK), BF16)], 0))
            out = dot(stacked[b], jnp.concatenate(sides, 1))
            mixed[2 * c, :, cols] = out[:, 0:BLK]
            mixed[2 * c + 1, :, cols] = out[:, BLK:2 * BLK]
        return carry

    lax.fori_loop(0, 8, mixing, 0)

    place = chosen.T[0:OY].astype(BF16)
    all_of(CONTRIB, rsem, spans[CONTRIB])
    for k in range(0, K, 2):
        pair = jnp.concatenate(
            [cin[:, n * CAP:(n + 1) * CAP, :].reshape(SLOTS, BLK) for n in (k, k + 1)], 1
        )
        hi, mid, lo = split3(pair)
        arrived = dot(place, hi) + dot(place, mid) + dot(place, lo)
        for n in range(2):
            old = oc[k + n, 0]
            new = old + ocean_uptake * wet * (arrived[:, n * BLK:(n + 1) * BLK] - old)
            oc[k + n, 0] = new
            lr[0, (k + n) * 4:(k + n) * 4 + 4, :] = new[0:HW]
            lr[1, (k + n) * 4:(k + n) * 4 + 4, :] = new[OY - HW:OY]
    groups = [
        (t, turned([oc[k, 0] for k in range(3 * t, min(3 * t + 3, K))])) for t in range(TRIPLES)
    ]
    cut_edges(groups, ls, lc, lane)
    late = halo(LATE, lr, lc, ls, lr_in, lc_in, ls_in, 4 * K)
    for copy in late:
        copy.start()


    all_of(EARLY, rsem, spans[EARLY])
    set_coefficients(coef, fields, er_in, outer_columns(es_in, ec_in, EARLY_GROUPS, lane), lane)
    for t in range(TRIPLES):
        ks = range(3 * t, min(3 * t + 3, K))
        for lev in range(1, OL):
            rows = [(k // 4) * 48 + (lev - 1) * 16 + (k % 4) * HW for k in ks]
            norths, souths = ([er_in[side, row:row + HW, :] for row in rows] for side in range(2))
            store_tile(
                state, coef, t, lev, widen([oc[k, lev] for k in ks], norths, souths),
                outer_columns(es_in, ec_in, t * 3 + lev - 1, lane),
            )

    acc[...] = jnp.zeros_like(acc)

    def return_group(t, carry):
        near = (8 - t) // 6
        u = (t + 6) % 9
        g = near * (3 + t) + (1 - near) * ((u // 2) * (1 - u % 2) + (8 - u // 2) * (u % 2))

        @pl.when(g != 4)
        def _():
            message(SURFACE, g, sbuf.at[g], sin.at[g], -1).wait_recv()

        parts = []
        for s in range(CAP):
            e = g * CAP + s
            hi, lo = split2(wbuf[jnp.maximum(inter[2, e], 0)])
            ahi, alo = split2(sin[g, pl.ds(s, K, stride=CAP), :])
            wets = jnp.broadcast_to(sin[g, pl.ds(K * CAP + s, 1), :], (K, BLK)).astype(BF16)
            lhs = jnp.concatenate([ahi, alo, wets], 0)
            first = dot(lhs, hi)
            second = dot(lhs, lo)
            parts.append((
                first[0:K] + first[K:2 * K] + second[0:K],
                first[2 * K:2 * K + 8] + second[2 * K:2 * K + 8],
            ))
        for b in range(ACB):
            tracers, wets = acc[b, 0:K, :], acc[b, K:K + 8, :]
            for s in range(CAP):
                e = g * CAP + s
                here = jnp.where((inter[0, e] == b) & (inter[1, e] >= 0), 1.0, 0.0).astype(F32)
                tracers = tracers + here * parts[s][0]
                wets = wets + here * parts[s][1]
            acc[b, 0:K, :] = tracers
            acc[b, K:K + 8, :] = wets
        return carry

    lax.fori_loop(0, 9, return_group, 0)
    for b in range(ACB):
        old = abuf[:, 0, b * BLK:(b + 1) * BLK]
        bottom[pl.ds(b, K, stride=ACB), :] = old + air_uptake * (
            acc[b, 0:K, :] - acc[b, K:K + 1, :] * old
        )

    all_of(LATE, rsem, spans[LATE])
    for t in range(TRIPLES):
        ks = range(3 * t, min(3 * t + 3, K))
        norths, souths = ([lr_in[side, k * HW:(k + 1) * HW, :] for k in ks] for side in range(2))
        store_tile(
            state, coef, t, 0, widen([oc[k, 0] for k in ks], norths, souths),
            outer_columns(ls_in, lc_in, t, lane),
        )

    for kind in range(5):
        all_of(kind, ssem, spans[kind])


def exchange(inter, atm, mix, oc, vel, mask, weights):
    vmem = pl.BlockSpec(memory_space=pltpu.VMEM)
    hbm = pl.BlockSpec(memory_space=pltpu.HBM)
    shapes = [
        (K, LA, ACB * BLK), (ACB, LA, BLK), (K * ACB, BLK),
        (7, COLS, BLK), (TRIPLES, OL, PADDED, BLK),
    ]
    halos = [
        (2, EARLY_ROWS, BLK), (4, 8, BLK), (2, EARLY_STRIP, BLK),
        (2, 4 * K, BLK), (4, 8, BLK), (2, LATE_STRIP, BLK),
    ]
    return pl.pallas_call(
        exchange_kernel,
        out_shape=[jax.ShapeDtypeStruct(s, F32) for s in shapes],
        in_specs=[hbm] * 7,
        out_specs=[vmem] * len(shapes),
        scratch_shapes=[
            pltpu.SMEM((3, SLOTS), jnp.int32),
            pltpu.VMEM((K, OL, OY, BLK), F32),
            pltpu.VMEM((3, OY, BLK), F32),
            pltpu.VMEM((WSL, BLK, BLK), F32),
            pltpu.VMEM((K, 8, ACB * BLK), F32),
            pltpu.VMEM((K, LA, ACB * BLK), F32),
            pltpu.VMEM((ACB, LA, LA), F32),
            pltpu.VMEM((OY, BLK), jnp.int32),
            pltpu.VMEM((ACB, LA, 2 * BLK), BF16),
            pltpu.VMEM((ACB, 2 * K, BLK), BF16),
            pltpu.VMEM((9, CAP, BLK), jnp.int32),
            pltpu.VMEM((9, CAP, BLK), jnp.int32),
            pltpu.VMEM((9, K * CAP, BLK), F32),
            pltpu.VMEM((9, K * CAP, BLK), F32),
            pltpu.VMEM((9, (K + 1) * CAP, BLK), F32),
            pltpu.VMEM((9, (K + 1) * CAP, BLK), F32),
            pltpu.VMEM((ACB, K + 8, BLK), F32),
            *[pltpu.VMEM(shape, F32) for shape in halos * 2],
            pltpu.SemaphoreType.DMA,
            pltpu.SemaphoreType.DMA,
            pltpu.SemaphoreType.DMA((6,)),
            pltpu.SemaphoreType.DMA((5,)),
            pltpu.SemaphoreType.DMA((5,)),
            pltpu.SemaphoreType.DMA((9,)),
        ],
        compiler_params=pltpu.CompilerParams(
            collective_id=0, has_side_effects=True, vmem_limit_bytes=30 * 2**20
        ),
        name="exchange",
    )(*(
        pltpu.with_memory_space_constraint(x, pltpu.HBM)
        for x in (inter, atm, mix, oc, vel, mask, weights)
    ))


def step_kernel(
    mixed, first_column, bottom, coef, state,
    atm_out, oc_out, atm_stage, oc_stage, work, asem, osem,
):
    def surface_part(k, carry):
        surface = bottom[pl.ds(pl.multiple_of(k * ACB, ACB), ACB), :]
        for b in range(ACB):
            cols = slice(b * BLK, (b + 1) * BLK)
            atm_stage[k, :, cols] = mixed[k, :, cols] + first_column[b] * surface[b:b + 1]
        pltpu.make_async_copy(atm_stage.at[k], atm_out.at[k], asem.at[k]).start()
        return carry

    lax.fori_loop(0, K, surface_part, 0)

    def ocean(t, carry):
        for sub in range(NSUB):
            def source(lev, start):
                if sub == 0:
                    return state[t, lev, start:start + 8, :]
                return work[(sub - 1) % 2, lev, start:start + 8, :]

            for tile in range(COLS // 8):
                start = 8 + tile * 8
                c = [coef[n, tile * 8:tile * 8 + 8, :] for n in range(6)]
                x = [source(lev, start) for lev in range(OL)]
                for lev in range(OL):
                    new = (
                        c[0] * source(lev, start + 1)
                        + c[1] * source(lev, start - 1)
                        + c[2] * pltpu.roll(x[lev], BLK - 1, 1)
                        + c[3] * pltpu.roll(x[lev], 1, 1)
                        + c[4] * (x[max(lev - 1, 0)] + x[min(lev + 1, OL - 1)])
                        + c[5] * x[lev]
                    )
                    work[sub % 2, lev, start:start + 8, :] = new
                    if tile == 0:
                        work[sub % 2, lev, 8 + COLS:PADDED, :] = new
                    if tile == COLS // 8 - 1:
                        work[sub % 2, lev, 0:8, :] = new
        for lev in range(OL):
            out = work[(NSUB - 1) % 2, lev, 8:8 + BLK, :].T
            for n in range(3):
                oc_stage[3 * t + n, lev] = out[n * LANES:n * LANES + OY]

        @pl.when(t < TRIPLES - 1)
        def _():
            pltpu.make_async_copy(
                oc_stage.at[pl.ds(3 * t, 3)], oc_out.at[pl.ds(3 * t, 3)], osem.at[t]
            ).start()

        return carry

    lax.fori_loop(0, TRIPLES, ocean, 0)
    last = pltpu.make_async_copy(
        oc_stage.at[pl.ds(K - 1, 1)], oc_out.at[pl.ds(K - 1, 1)], osem.at[TRIPLES - 1]
    )
    last.start()
    for k in range(K):
        pltpu.make_async_copy(atm_stage.at[k], atm_out.at[k], asem.at[k]).wait()
    for t in range(TRIPLES - 1):
        pltpu.make_async_copy(
            oc_stage.at[pl.ds(3 * t, 3)], oc_out.at[pl.ds(3 * t, 3)], osem.at[t]
        ).wait()
    last.wait()


def local_step(arrays):
    vmem = pl.BlockSpec(memory_space=pltpu.VMEM)
    hbm = pl.BlockSpec(memory_space=pltpu.HBM)
    return pl.pallas_call(
        step_kernel,
        out_shape=[
            jax.ShapeDtypeStruct((K, LA, ACB * BLK), F32),
            jax.ShapeDtypeStruct((K, OL, OY, BLK), F32),
        ],
        in_specs=[vmem] * len(arrays),
        out_specs=[hbm, hbm],
        scratch_shapes=[
            pltpu.VMEM((K, LA, ACB * BLK), F32),
            pltpu.VMEM((3 * TRIPLES, OL, OY, BLK), F32),
            pltpu.VMEM((2, OL, PADDED, BLK), F32),
            pltpu.SemaphoreType.DMA((K,)),
            pltpu.SemaphoreType.DMA((TRIPLES,)),
        ],
        compiler_params=pltpu.CompilerParams(vmem_limit_bytes=20 * 2**20),
        name="step",
    )(*arrays)


def body(atm, mix, oc, vel, mask, inter, weights):
    return tuple(local_step(exchange(inter, atm, mix, oc, vel, mask, weights)))


def solution(mesh):
    in_specs = (
        P(None, None, ("gx", "gy")),
        P(("gx", "gy"), None, None),
        P(None, None, "gy", "gx"),
        P(None, "gy", "gx"),
        P("gy", "gx"),
        P(None, ("gx", "gy")),
        P(("gx", "gy"), None, None),
    )
    out_specs = (P(None, None, ("gx", "gy")), P(None, None, "gy", "gx"))
    return jax.shard_map(body, mesh=mesh, in_specs=in_specs, out_specs=out_specs, check_vma=False)
```

```python
import functools

import jax
import jax.numpy as jnp
from jax import lax
from jax.experimental import pallas as pl
from jax.experimental.pallas import tpu as pltpu
from jax.sharding import PartitionSpec as P

K = 16
LA = 72
OL = 4
OY = 32
BLK = 128
ACB = 8
CAP = 8
WSL = 64
NSUB = 4
SLOTS = 9 * CAP
HW = NSUB
LANES = OY + 2 * HW
TRIPLES = 6
EARLY_GROUPS = TRIPLES * (OL - 1)
COLS = BLK + 2 * HW
PADDED = COLS + 16

ocean_uptake = 0.5
air_uptake = 0.5
mix_horizontal = 0.15
mix_vertical = 0.2

F32 = jnp.float32
BF16 = jnp.bfloat16
MESH = pl.DeviceIdType.MESH
NEIGHBOURS = (0, 8, 1, 7, 2, 6, 3, 5)
REQUEST, CONTRIB, SURFACE, EARLY, LATE = range(5)
NQ = 4
EARLY_ROWS = NQ * 48 + 16
EARLY_STRIP = 96
LATE_STRIP = 24


def split2(x):
    hi = x.astype(BF16)
    return hi, (x - hi.astype(F32)).astype(BF16)


def split3(x):
    hi = x.astype(BF16)
    rest = x - hi.astype(F32)
    mid = rest.astype(BF16)
    return hi, mid, (rest - mid.astype(F32)).astype(BF16)


def dot(a, b):
    return jnp.dot(a, b, preferred_element_type=F32)


def dot_nt(a, b):
    return lax.dot_general(a, b, (((1,), (1,)), ((), ())), preferred_element_type=F32)


def turned(tiles):
    gap = jnp.zeros((2 * HW, BLK), F32)
    rows = []
    for tile in tiles:
        rows += [tile, gap]
    full = jnp.concatenate(rows, 0)
    if full.shape[0] < BLK:
        full = jnp.concatenate([full, jnp.zeros((BLK - full.shape[0], BLK), F32)], 0)
    return full.T


def cut_edges(groups, strips, ends, lane):
    blocks = {}
    for n, full in groups:
        strips[0, n * HW:(n + 1) * HW, :] = full[0:HW]
        strips[1, n * HW:(n + 1) * HW, :] = full[BLK - HW:BLK]
        edge = jnp.concatenate([full[0:HW], full[BLK - HW:BLK]], 0)
        here = (lane % LANES) // HW == n % 10
        low = pltpu.roll(edge, (n % 10) * HW, 1)
        high = pltpu.roll(edge, ((n % 10) * HW - (OY - HW)) % BLK, 1)
        old = blocks.get(n // 10, (jnp.zeros((8, BLK), F32),) * 2)
        blocks[n // 10] = (jnp.where(here, low, old[0]), jnp.where(here, high, old[1]))
    for b in range(2):
        low, high = blocks.get(b, (jnp.zeros((8, BLK), F32),) * 2)
        rows = slice(b * HW, (b + 1) * HW)
        ends[0, rows, :] = low[0:HW]
        ends[1, rows, :] = low[HW:8]
        ends[2, rows, :] = high[0:HW]
        ends[3, rows, :] = high[HW:8]


def widen(tiles, norths, souths):
    gap = jnp.zeros((HW, BLK), F32)
    rows = []
    for n in range(3):
        n_row = norths[n] if n < len(tiles) else gap
        s_row = souths[n + 1] if n + 1 < len(tiles) else gap
        rows += [tiles[n] if n < len(tiles) else jnp.zeros((OY, BLK), F32), n_row, s_row]
    return jnp.concatenate(rows + [gap, souths[0]], 0).T


def outer_columns(strips, ends, n, lane):
    shifted = (lane + HW) % BLK
    north = (shifted % LANES >= OY + HW) & (shifted < 3 * LANES)
    south = (shifted % LANES < HW) & (shifted < 3 * LANES)
    rows = slice((n // 10) * HW, (n // 10 + 1) * HW)
    mine = jnp.concatenate(
        [strips[0, n * HW:(n + 1) * HW, :], strips[1, n * HW:(n + 1) * HW, :]], 0
    )
    above = jnp.concatenate([ends[0, rows, :], ends[1, rows, :]], 0)
    below = jnp.concatenate([ends[2, rows, :], ends[3, rows, :]], 0)
    above = pltpu.roll(above, (OY - (n % 10) * HW) % BLK, 1)
    below = pltpu.roll(below, (BLK - HW - (n % 10) * HW) % BLK, 1)
    return jnp.where(north, above, jnp.where(south, below, mine))


def store_tile(state, coef, t, lev, inner, outer):
    inner = inner * coef[6, 0:BLK, :]
    outer = outer * coef[6, BLK:COLS, :]
    state[t, lev, 0:8, :] = outer
    state[t, lev, 8:8 + BLK, :] = inner
    state[t, lev, 8 + BLK:8 + COLS, :] = outer
    state[t, lev, 8 + COLS:PADDED, :] = inner[0:8]


def set_coefficients(coef, own, er, ends, lane):
    shifted = (lane + HW) % BLK
    fields = []
    for n in range(3):
        row = NQ * 48 + n * HW
        inner = widen([own[n]] * 3, [er[0, row:row + HW, :]] * 3, [er[1, row:row + HW, :]] * 3)
        parts = [pltpu.roll(ends, ((m - n) * LANES) % BLK, 1) for m in range(3)]
        outer = jnp.where(
            shifted < LANES, parts[0], jnp.where(shifted < 2 * LANES, parts[1], parts[2])
        )
        fields.append(jnp.concatenate([inner, outer], 0))
    u, v, wet = fields
    coef[0] = wet * (mix_horizontal - 0.5 * u)
    coef[1] = wet * (mix_horizontal + 0.5 * u)
    coef[2] = wet * (mix_horizontal - 0.5 * v)
    coef[3] = wet * (mix_horizontal + 0.5 * v)
    coef[4] = wet * mix_vertical
    coef[5] = wet * (1.0 - 4.0 * mix_horizontal - 2.0 * mix_vertical)
    coef[6] = wet


def exchange_kernel(
    inter_hbm, atm_hbm, mix_hbm, oc_hbm, vel_hbm, mask_hbm, w_hbm,
    mixed, first_column, bottom, coef, state,
    inter, oc, fields, wbuf, abuf, xbuf, mbuf, maskbuf, stacked, ast,
    req, reqs, cbuf, cin, sbuf, sin, acc,
    er, ec, es, lr, lc, ls, er_in, ec_in, es_in, lr_in, lc_in, ls_in,
    wsem, xsem, lsem, ssem, rsem, surf_sem,
):
    nx, ny = lax.axis_size("gx"), lax.axis_size("gy")
    i, j = lax.axis_index("gx"), lax.axis_index("gy")

    def device(g, sign):
        dy, dx = g // 3 - 1, g % 3 - 1
        return ((i + sign * dx + nx) % nx, (j + sign * dy + ny) % ny)

    def message(kind, g, src, dst, sign=1):
        return pltpu.make_async_remote_copy(
            src_ref=src, dst_ref=dst, send_sem=ssem.at[kind],
            recv_sem=surf_sem.at[g] if kind == SURFACE else rsem.at[kind],
            device_id=device(g, sign), device_id_type=MESH,
        )

    def all_of(kind, sem, span):
        pltpu.make_async_copy(span, span, sem.at[kind]).wait()

    spans = {
        REQUEST: req.at[pl.ds(0, 8)], CONTRIB: cbuf.at[pl.ds(0, 8)], SURFACE: sbuf.at[pl.ds(0, 8)],
        EARLY: wbuf.at[pl.ds(0, 5)], LATE: er.at[0],
    }

    barrier = pltpu.get_barrier_semaphore()
    for g in NEIGHBOURS:
        pl.semaphore_signal(barrier, inc=1, device_id=device(g, 1), device_id_type=MESH)

    small = [
        pltpu.make_async_copy(src, dst, lsem.at[n])
        for n, (src, dst) in enumerate((
            (oc_hbm, oc), (vel_hbm, fields.at[pl.ds(0, 2)]), (mask_hbm, maskbuf),
            (atm_hbm.at[:, pl.ds(0, 8), :], abuf), (mix_hbm, mbuf), (inter_hbm, inter),
        ))
    ]
    weights = pltpu.make_async_copy(w_hbm, wbuf, wsem)
    columns = pltpu.make_async_copy(atm_hbm, xbuf, xsem)
    small[5].start()
    small[3].start()
    weights.start()

    small[5].wait()
    for e in range(SLOTS):
        req[e // CAP, pl.ds(e % CAP, 1), :] = jnp.full((1, BLK), inter[1, e], jnp.int32)
    reqs[4] = req[4]

    small[3].wait()
    for b in range(ACB):
        block = abuf[:, 0, b * BLK:(b + 1) * BLK]
        hi, lo = split2(block)
        ast[b, 0:K, :] = hi
        ast[b, K:2 * K, :] = lo
    for load in small[0:3] + small[4:5]:
        load.start()
    weights.wait()
    columns.start()

    def contrib_rows(g):
        for s in range(CAP):
            e = g * CAP + s
            hi, lo = split2(wbuf[jnp.maximum(inter[2, e], 0)])
            a = ast[jnp.maximum(inter[0, e], 0)]
            first = dot_nt(a, hi)
            second = dot_nt(a[0:K], lo)
            cbuf[g, pl.ds(s, K, stride=CAP), :] = first[0:K] + first[K:2 * K] + second

    contrib_rows(NEIGHBOURS[0])
    pl.semaphore_wait(barrier, len(NEIGHBOURS))

    requests = [message(REQUEST, g, req.at[g], reqs.at[g]) for g in NEIGHBOURS]
    for copy in requests:
        copy.start()

    message(CONTRIB, NEIGHBOURS[0], cbuf.at[NEIGHBOURS[0]], cin.at[NEIGHBOURS[0]]).start()

    def contrib_group(t, carry):
        g = (t // 2) * (1 - t % 2) + (8 - t // 2) * (t % 2)
        contrib_rows(g)

        @pl.when(g != 4)
        def _():
            message(CONTRIB, g, cbuf.at[g], cin.at[g]).start()

        return carry

    lax.fori_loop(1, 9, contrib_group, 0)
    cin[4] = cbuf[4]

    for load in small[0:3]:
        load.wait()
    wet = maskbuf[...].astype(F32)
    fields[2] = wet
    vel = fields

    er[:, NQ * 48 + 8:EARLY_ROWS, :] = jnp.zeros((2, 8, BLK), F32)
    es[:, 72:EARLY_STRIP, :] = jnp.zeros((2, EARLY_STRIP - 72, BLK), F32)
    lane = lax.broadcasted_iota(jnp.int32, (8, BLK), 1)
    for q in range(NQ):
        for lev in range(1, OL):
            for p in range(4):
                row = q * 48 + (lev - 1) * 16 + p * 4
                er[0, row:row + HW, :] = oc[4 * q + p, lev, 0:HW, :]
                er[1, row:row + HW, :] = oc[4 * q + p, lev, OY - HW:OY, :]
    for n in range(3):
        row = NQ * 48 + n * 4
        field = vel[n] if n < 2 else wet
        er[0, row:row + HW, :] = field[0:HW]
        er[1, row:row + HW, :] = field[OY - HW:OY]
    groups = [
        (t * 3 + lev - 1, turned([oc[k, lev] for k in range(3 * t, min(3 * t + 3, K))]))
        for t in range(TRIPLES) for lev in range(1, OL)
    ]
    cut_edges(groups + [(EARLY_GROUPS, turned([vel[0], vel[1], wet]))], es, ec, lane)

    sides = {1: 0, 7: 1}
    ends = {3: 0, 5: 1}
    corners = {0: 0, 2: 1, 6: 2, 8: 3}

    def halo(kind, rows, corner, strip, rows_in, corner_in, strip_in, count):
        copies = []
        for g in NEIGHBOURS:
            if g in sides:
                n = sides[g]
                copies.append(message(kind, g, rows.at[n, pl.ds(0, count)], rows_in.at[n]))
            elif g in ends:
                n = ends[g]
                copies.append(message(kind, g, strip.at[n], strip_in.at[n]))
            else:
                n = corners[g]
                copies.append(message(kind, g, corner.at[n], corner_in.at[n]))
        return copies

    early = halo(EARLY, er, ec, es, er_in, ec_in, es_in, EARLY_ROWS)
    for copy in early:
        copy.start()

    all_of(REQUEST, rsem, spans[REQUEST])
    lanes = lax.broadcasted_iota(jnp.int32, (SLOTS, BLK), 1)
    chosen = (reqs[...].reshape(SLOTS, BLK) == lanes).astype(F32)
    pick = chosen[:, 0:OY].astype(BF16)
    for k in range(0, K, 2):
        pair = jnp.concatenate([oc[k, 0] * wet, oc[k + 1, 0] * wet], 1)
        hi, mid, lo = split3(pair)
        rows = dot(pick, hi) + dot(pick, mid) + dot(pick, lo)
        for g in range(9):
            sbuf[g, k * CAP:(k + 1) * CAP, :] = rows[g * CAP:(g + 1) * CAP, 0:BLK]
            sbuf[g, (k + 1) * CAP:(k + 2) * CAP, :] = rows[g * CAP:(g + 1) * CAP, BLK:2 * BLK]
    rows = dot(pick, wet.astype(BF16))
    for g in range(9):
        sbuf[g, K * CAP:(K + 1) * CAP, :] = rows[g * CAP:(g + 1) * CAP]
    sin[4] = sbuf[4]
    for g in NEIGHBOURS:
        message(SURFACE, g, sbuf.at[g], sin.at[g], -1).start()

    small[4].wait()
    for b in range(ACB):
        m = jnp.concatenate([mbuf[b], jnp.zeros((LA, 2 * BLK - LA), F32)], 1)
        first_column[b] = jnp.broadcast_to(m[:, 0:1], (LA, BLK))
        mh = m.astype(BF16).astype(F32)
        stacked[b] = (mh + pltpu.roll(mh, 80, 1) + pltpu.roll(m - mh, 160, 1)).astype(BF16)
    upper = lax.broadcasted_iota(jnp.int32, (8, BLK), 0) > 0

    columns.wait()

    def mixing(c, carry):
        for b in range(ACB):
            cols = slice(b * BLK, (b + 1) * BLK)
            sides = []
            for n in range(2):
                x = jnp.concatenate([
                    jnp.where(upper, xbuf[2 * c + n, 0:8, cols], 0.0),
                    xbuf[2 * c + n, 8:LA, cols],
                    jnp.zeros((8, BLK), F32),
                ], 0)
                hi, lo = split2(x)
                sides.append(jnp.concatenate([hi, lo, hi, jnp.zeros((16, BLK), BF16)], 0))
            out = dot(stacked[b], jnp.concatenate(sides, 1))
            mixed[2 * c, :, cols] = out[:, 0:BLK]
            mixed[2 * c + 1, :, cols] = out[:, BLK:2 * BLK]
        return carry

    lax.fori_loop(0, 8, mixing, 0)

    place = chosen.T[0:OY].astype(BF16)
    all_of(CONTRIB, rsem, spans[CONTRIB])
    for k in range(0, K, 2):
        pair = jnp.concatenate(
            [cin[:, n * CAP:(n + 1) * CAP, :].reshape(SLOTS, BLK) for n in (k, k + 1)], 1
        )
        hi, mid, lo = split3(pair)
        arrived = dot(place, hi) + dot(place, mid) + dot(place, lo)
        for n in range(2):
            old = oc[k + n, 0]
            new = old + ocean_uptake * wet * (arrived[:, n * BLK:(n + 1) * BLK] - old)
            oc[k + n, 0] = new
            lr[0, (k + n) * 4:(k + n) * 4 + 4, :] = new[0:HW]
            lr[1, (k + n) * 4:(k + n) * 4 + 4, :] = new[OY - HW:OY]
    groups = [
        (t, turned([oc[k, 0] for k in range(3 * t, min(3 * t + 3, K))])) for t in range(TRIPLES)
    ]
    cut_edges(groups, ls, lc, lane)
    late = halo(LATE, lr, lc, ls, lr_in, lc_in, ls_in, 4 * K)
    for copy in late:
        copy.start()


    all_of(EARLY, rsem, spans[EARLY])
    set_coefficients(coef, fields, er_in, outer_columns(es_in, ec_in, EARLY_GROUPS, lane), lane)
    for t in range(TRIPLES):
        ks = range(3 * t, min(3 * t + 3, K))
        for lev in range(1, OL):
            rows = [(k // 4) * 48 + (lev - 1) * 16 + (k % 4) * HW for k in ks]
            norths, souths = ([er_in[side, row:row + HW, :] for row in rows] for side in range(2))
            store_tile(
                state, coef, t, lev, widen([oc[k, lev] for k in ks], norths, souths),
                outer_columns(es_in, ec_in, t * 3 + lev - 1, lane),
            )

    acc[...] = jnp.zeros_like(acc)

    def return_group(t, carry):
        near = (8 - t) // 6
        u = (t + 6) % 9
        g = near * (3 + t) + (1 - near) * ((u // 2) * (1 - u % 2) + (8 - u // 2) * (u % 2))

        @pl.when(g != 4)
        def _():
            message(SURFACE, g, sbuf.at[g], sin.at[g], -1).wait_recv()

        parts = []
        for s in range(CAP):
            e = g * CAP + s
            hi, lo = split2(wbuf[jnp.maximum(inter[2, e], 0)])
            ahi, alo = split2(sin[g, pl.ds(s, K, stride=CAP), :])
            wets = jnp.broadcast_to(sin[g, pl.ds(K * CAP + s, 1), :], (K, BLK)).astype(BF16)
            lhs = jnp.concatenate([ahi, alo, wets], 0)
            first = dot(lhs, hi)
            second = dot(lhs, lo)
            parts.append((
                first[0:K] + first[K:2 * K] + second[0:K],
                first[2 * K:2 * K + 8] + second[2 * K:2 * K + 8],
            ))
        for b in range(ACB):
            tracers, wets = acc[b, 0:K, :], acc[b, K:K + 8, :]
            for s in range(CAP):
                e = g * CAP + s
                here = jnp.where((inter[0, e] == b) & (inter[1, e] >= 0), 1.0, 0.0).astype(F32)
                tracers = tracers + here * parts[s][0]
                wets = wets + here * parts[s][1]
            acc[b, 0:K, :] = tracers
            acc[b, K:K + 8, :] = wets
        return carry

    lax.fori_loop(0, 9, return_group, 0)
    for b in range(ACB):
        old = abuf[:, 0, b * BLK:(b + 1) * BLK]
        bottom[pl.ds(b, K, stride=ACB), :] = old + air_uptake * (
            acc[b, 0:K, :] - acc[b, K:K + 1, :] * old
        )

    all_of(LATE, rsem, spans[LATE])
    for t in range(TRIPLES):
        ks = range(3 * t, min(3 * t + 3, K))
        norths, souths = ([lr_in[side, k * HW:(k + 1) * HW, :] for k in ks] for side in range(2))
        store_tile(
            state, coef, t, 0, widen([oc[k, 0] for k in ks], norths, souths),
            outer_columns(ls_in, lc_in, t, lane),
        )

    for kind in range(5):
        all_of(kind, ssem, spans[kind])


def exchange(inter, atm, mix, oc, vel, mask, weights):
    vmem = pl.BlockSpec(memory_space=pltpu.VMEM)
    hbm = pl.BlockSpec(memory_space=pltpu.HBM)
    shapes = [
        (K, LA, ACB * BLK), (ACB, LA, BLK), (K * ACB, BLK),
        (7, COLS, BLK), (TRIPLES, OL, PADDED, BLK),
    ]
    halos = [
        (2, EARLY_ROWS, BLK), (4, 8, BLK), (2, EARLY_STRIP, BLK),
        (2, 4 * K, BLK), (4, 8, BLK), (2, LATE_STRIP, BLK),
    ]
    return pl.pallas_call(
        exchange_kernel,
        out_shape=[jax.ShapeDtypeStruct(s, F32) for s in shapes],
        in_specs=[hbm] * 7,
        out_specs=[vmem] * len(shapes),
        scratch_shapes=[
            pltpu.SMEM((3, SLOTS), jnp.int32),
            pltpu.VMEM((K, OL, OY, BLK), F32),
            pltpu.VMEM((3, OY, BLK), F32),
            pltpu.VMEM((WSL, BLK, BLK), F32),
            pltpu.VMEM((K, 8, ACB * BLK), F32),
            pltpu.VMEM((K, LA, ACB * BLK), F32),
            pltpu.VMEM((ACB, LA, LA), F32),
            pltpu.VMEM((OY, BLK), jnp.int32),
            pltpu.VMEM((ACB, LA, 2 * BLK), BF16),
            pltpu.VMEM((ACB, 2 * K, BLK), BF16),
            pltpu.VMEM((9, CAP, BLK), jnp.int32),
            pltpu.VMEM((9, CAP, BLK), jnp.int32),
            pltpu.VMEM((9, K * CAP, BLK), F32),
            pltpu.VMEM((9, K * CAP, BLK), F32),
            pltpu.VMEM((9, (K + 1) * CAP, BLK), F32),
            pltpu.VMEM((9, (K + 1) * CAP, BLK), F32),
            pltpu.VMEM((ACB, K + 8, BLK), F32),
            *[pltpu.VMEM(shape, F32) for shape in halos * 2],
            pltpu.SemaphoreType.DMA,
            pltpu.SemaphoreType.DMA,
            pltpu.SemaphoreType.DMA((6,)),
            pltpu.SemaphoreType.DMA((5,)),
            pltpu.SemaphoreType.DMA((5,)),
            pltpu.SemaphoreType.DMA((9,)),
        ],
        compiler_params=pltpu.CompilerParams(
            collective_id=0, has_side_effects=True, vmem_limit_bytes=30 * 2**20
        ),
        name="exchange",
    )(*(
        pltpu.with_memory_space_constraint(x, pltpu.HBM)
        for x in (inter, atm, mix, oc, vel, mask, weights)
    ))


def step_kernel(
    mixed, first_column, bottom, coef, state,
    atm_out, oc_out, atm_stage, oc_stage, work, shift, asem, osem,
):
    row = lax.broadcasted_iota(jnp.int32, (2 * BLK, 2 * BLK), 0) % BLK
    col = lax.broadcasted_iota(jnp.int32, (2 * BLK, 2 * BLK), 1)
    step = jnp.where(col < BLK, 1, BLK - 1)
    shift[...] = (row == (col + step) % BLK).astype(F32).astype(BF16)

    def ocean(t, carry):
        for n in range(3):
            k = jnp.minimum(3 * t + n, K - 1)
            surface = bottom[pl.ds(pl.multiple_of(k * ACB, ACB), ACB), :]
            for b in range(ACB):
                cols = slice(b * BLK, (b + 1) * BLK)
                atm_stage[3 * t + n, :, cols] = (
                    mixed[k, :, cols] + first_column[b] * surface[b:b + 1]
                )
        for sub in range(NSUB):
            def source(lev, start):
                if sub == 0:
                    return state[t, lev, start:start + 8, :]
                return work[(sub - 1) % 2, lev, start:start + 8, :]

            bottom_level = OL - 1
            whole = jnp.concatenate(
                [source(bottom_level, 8 + tile * 8) for tile in range(COLS // 8 + 1)], 0
            )
            moved = dot(jnp.concatenate(split2(whole), 1), shift[...])

            for tile, levels in (
                [(tile, range(bottom_level)) for tile in range(COLS // 8)]
                + [(tile, [bottom_level]) for tile in range(COLS // 8)]
            ):
                start = 8 + tile * 8
                c = [coef[n, tile * 8:tile * 8 + 8, :] for n in range(6)]
                x = {
                    lev: source(lev, start)
                    for lev in range(max(levels[0] - 1, 0), min(levels[-1] + 2, OL))
                }
                for lev in levels:
                    if lev == bottom_level:
                        north = moved[tile * 8:tile * 8 + 8, 0:BLK]
                        south = moved[tile * 8:tile * 8 + 8, BLK:2 * BLK]
                    else:
                        north = pltpu.roll(x[lev], BLK - 1, 1)
                        south = pltpu.roll(x[lev], 1, 1)
                    new = (
                        c[0] * source(lev, start + 1)
                        + c[1] * source(lev, start - 1)
                        + c[2] * north
                        + c[3] * south
                        + c[4] * (x[max(lev - 1, 0)] + x[min(lev + 1, OL - 1)])
                        + c[5] * x[lev]
                    )
                    work[sub % 2, lev, start:start + 8, :] = new
                    if tile == 0:
                        work[sub % 2, lev, 8 + COLS:PADDED, :] = new
                    if tile == COLS // 8 - 1:
                        work[sub % 2, lev, 0:8, :] = new
        for lev in range(OL):
            out = work[(NSUB - 1) % 2, lev, 8:8 + BLK, :].T
            for n in range(3):
                oc_stage[3 * t + n, lev] = out[n * LANES:n * LANES + OY]

        @pl.when(t < TRIPLES - 1)
        def _():
            three = pl.ds(3 * t, 3)
            pltpu.make_async_copy(atm_stage.at[three], atm_out.at[three], asem.at[t]).start()
            pltpu.make_async_copy(oc_stage.at[three], oc_out.at[three], osem.at[t]).start()

        return carry

    lax.fori_loop(0, TRIPLES, ocean, 0)
    copies = [
        pltpu.make_async_copy(stage.at[part], out.at[part], sem.at[TRIPLES - 1])
        for part in [pl.ds(K - 1, 1)]
        for stage, out, sem in ((atm_stage, atm_out, asem), (oc_stage, oc_out, osem))
    ]
    for copy in copies:
        copy.start()
    for t in range(TRIPLES - 1):
        three = pl.ds(3 * t, 3)
        pltpu.make_async_copy(atm_stage.at[three], atm_out.at[three], asem.at[t]).wait()
        pltpu.make_async_copy(oc_stage.at[three], oc_out.at[three], osem.at[t]).wait()
    for copy in copies:
        copy.wait()


def local_step(arrays):
    vmem = pl.BlockSpec(memory_space=pltpu.VMEM)
    hbm = pl.BlockSpec(memory_space=pltpu.HBM)
    return pl.pallas_call(
        step_kernel,
        out_shape=[
            jax.ShapeDtypeStruct((K, LA, ACB * BLK), F32),
            jax.ShapeDtypeStruct((K, OL, OY, BLK), F32),
        ],
        in_specs=[vmem] * len(arrays),
        out_specs=[hbm, hbm],
        scratch_shapes=[
            pltpu.VMEM((3 * TRIPLES, LA, ACB * BLK), F32),
            pltpu.VMEM((3 * TRIPLES, OL, OY, BLK), F32),
            pltpu.VMEM((2, OL, PADDED, BLK), F32),
            pltpu.VMEM((2 * BLK, 2 * BLK), BF16),
            pltpu.SemaphoreType.DMA((TRIPLES,)),
            pltpu.SemaphoreType.DMA((TRIPLES,)),
        ],
        compiler_params=pltpu.CompilerParams(vmem_limit_bytes=20 * 2**20),
        name="step",
    )(*arrays)


def body(atm, mix, oc, vel, mask, inter, weights):
    return tuple(local_step(exchange(inter, atm, mix, oc, vel, mask, weights)))


def solution(mesh):
    in_specs = (
        P(None, None, ("gx", "gy")),
        P(("gx", "gy"), None, None),
        P(None, None, "gy", "gx"),
        P(None, "gy", "gx"),
        P("gy", "gx"),
        P(None, ("gx", "gy")),
        P(("gx", "gy"), None, None),
    )
    out_specs = (P(None, None, ("gx", "gy")), P(None, None, "gy", "gx"))
    return jax.shard_map(body, mesh=mesh, in_specs=in_specs, out_specs=out_specs, check_vma=False)
```

```python
import functools

import jax
import jax.numpy as jnp
from jax import lax
from jax.experimental import pallas as pl
from jax.experimental.pallas import tpu as pltpu
from jax.sharding import PartitionSpec as P

K = 16
LA = 72
OL = 4
OY = 32
BLK = 128
ACB = 8
CAP = 8
WSL = 64
NSUB = 4
SLOTS = 9 * CAP
HW = NSUB
LANES = OY + 2 * HW
TRIPLES = 6
EARLY_GROUPS = TRIPLES * (OL - 1)
COLS = BLK + 2 * HW
PADDED = COLS + 16

ocean_uptake = 0.5
air_uptake = 0.5
mix_horizontal = 0.15
mix_vertical = 0.2

F32 = jnp.float32
BF16 = jnp.bfloat16
MESH = pl.DeviceIdType.MESH
NEIGHBOURS = (0, 8, 1, 7, 2, 6, 3, 5)
REQUEST, CONTRIB, SURFACE, EARLY, LATE = range(5)
NQ = 4
EARLY_ROWS = NQ * 48 + 16
EARLY_STRIP = 96
LATE_STRIP = 24


def split2(x):
    hi = x.astype(BF16)
    return hi, (x - hi.astype(F32)).astype(BF16)


def split3(x):
    hi = x.astype(BF16)
    rest = x - hi.astype(F32)
    mid = rest.astype(BF16)
    return hi, mid, (rest - mid.astype(F32)).astype(BF16)


def dot(a, b):
    return jnp.dot(a, b, preferred_element_type=F32)


def dot_nt(a, b):
    return lax.dot_general(a, b, (((1,), (1,)), ((), ())), preferred_element_type=F32)


def turned(tiles):
    gap = jnp.zeros((2 * HW, BLK), F32)
    rows = []
    for tile in tiles:
        rows += [tile, gap]
    full = jnp.concatenate(rows, 0)
    if full.shape[0] < BLK:
        full = jnp.concatenate([full, jnp.zeros((BLK - full.shape[0], BLK), F32)], 0)
    return full.T


def cut_edges(groups, strips, ends, lane):
    blocks = {}
    for n, full in groups:
        strips[0, n * HW:(n + 1) * HW, :] = full[0:HW]
        strips[1, n * HW:(n + 1) * HW, :] = full[BLK - HW:BLK]
        edge = jnp.concatenate([full[0:HW], full[BLK - HW:BLK]], 0)
        here = (lane % LANES) // HW == n % 10
        low = pltpu.roll(edge, (n % 10) * HW, 1)
        high = pltpu.roll(edge, ((n % 10) * HW - (OY - HW)) % BLK, 1)
        old = blocks.get(n // 10, (jnp.zeros((8, BLK), F32),) * 2)
        blocks[n // 10] = (jnp.where(here, low, old[0]), jnp.where(here, high, old[1]))
    for b in range(2):
        low, high = blocks.get(b, (jnp.zeros((8, BLK), F32),) * 2)
        rows = slice(b * HW, (b + 1) * HW)
        ends[0, rows, :] = low[0:HW]
        ends[1, rows, :] = low[HW:8]
        ends[2, rows, :] = high[0:HW]
        ends[3, rows, :] = high[HW:8]


def widen(tiles, norths, souths):
    gap = jnp.zeros((HW, BLK), F32)
    rows = []
    for n in range(3):
        n_row = norths[n] if n < len(tiles) else gap
        s_row = souths[n + 1] if n + 1 < len(tiles) else gap
        rows += [tiles[n] if n < len(tiles) else jnp.zeros((OY, BLK), F32), n_row, s_row]
    return jnp.concatenate(rows + [gap, souths[0]], 0).T


def outer_columns(strips, ends, n, lane):
    shifted = (lane + HW) % BLK
    north = (shifted % LANES >= OY + HW) & (shifted < 3 * LANES)
    south = (shifted % LANES < HW) & (shifted < 3 * LANES)
    rows = slice((n // 10) * HW, (n // 10 + 1) * HW)
    mine = jnp.concatenate(
        [strips[0, n * HW:(n + 1) * HW, :], strips[1, n * HW:(n + 1) * HW, :]], 0
    )
    above = jnp.concatenate([ends[0, rows, :], ends[1, rows, :]], 0)
    below = jnp.concatenate([ends[2, rows, :], ends[3, rows, :]], 0)
    above = pltpu.roll(above, (OY - (n % 10) * HW) % BLK, 1)
    below = pltpu.roll(below, (BLK - HW - (n % 10) * HW) % BLK, 1)
    return jnp.where(north, above, jnp.where(south, below, mine))


def store_tile(state, coef, t, lev, inner, outer):
    inner = inner * coef[6, 0:BLK, :]
    outer = outer * coef[6, BLK:COLS, :]
    state[t, lev, 0:8, :] = outer
    state[t, lev, 8:8 + BLK, :] = inner
    state[t, lev, 8 + BLK:8 + COLS, :] = outer
    state[t, lev, 8 + COLS:PADDED, :] = inner[0:8]


def set_coefficients(coef, own, er, ends, lane):
    shifted = (lane + HW) % BLK
    fields = []
    for n in range(3):
        row = NQ * 48 + n * HW
        inner = widen([own[n]] * 3, [er[0, row:row + HW, :]] * 3, [er[1, row:row + HW, :]] * 3)
        parts = [pltpu.roll(ends, ((m - n) * LANES) % BLK, 1) for m in range(3)]
        outer = jnp.where(
            shifted < LANES, parts[0], jnp.where(shifted < 2 * LANES, parts[1], parts[2])
        )
        fields.append(jnp.concatenate([inner, outer], 0))
    u, v, wet = fields
    coef[0] = wet * (mix_horizontal - 0.5 * u)
    coef[1] = wet * (mix_horizontal + 0.5 * u)
    coef[2] = wet * (mix_horizontal - 0.5 * v)
    coef[3] = wet * (mix_horizontal + 0.5 * v)
    coef[4] = wet * mix_vertical
    coef[5] = wet * (1.0 - 4.0 * mix_horizontal - 2.0 * mix_vertical)
    coef[6] = wet


def exchange_kernel(
    inter_hbm, atm_hbm, mix_hbm, oc_hbm, vel_hbm, mask_hbm, w_hbm,
    mixed, first_column, bottom, coef, state,
    inter, oc, fields, wbuf, abuf, xbuf, mbuf, maskbuf, stacked, ast,
    req, reqs, cbuf, cin, sbuf, sin, acc,
    er, ec, es, lr, lc, ls, er_in, ec_in, es_in, lr_in, lc_in, ls_in,
    wsem, xsem, lsem, ssem, rsem, surf_sem,
):
    nx, ny = lax.axis_size("gx"), lax.axis_size("gy")
    i, j = lax.axis_index("gx"), lax.axis_index("gy")

    def device(g, sign):
        dy, dx = g // 3 - 1, g % 3 - 1
        return ((i + sign * dx + nx) % nx, (j + sign * dy + ny) % ny)

    def message(kind, g, src, dst, sign=1):
        return pltpu.make_async_remote_copy(
            src_ref=src, dst_ref=dst, send_sem=ssem.at[kind],
            recv_sem=surf_sem.at[g] if kind == SURFACE else rsem.at[kind],
            device_id=device(g, sign), device_id_type=MESH,
        )

    def all_of(kind, sem, span):
        pltpu.make_async_copy(span, span, sem.at[kind]).wait()

    spans = {
        REQUEST: req.at[pl.ds(0, 8)], CONTRIB: cbuf.at[pl.ds(0, 8)], SURFACE: sbuf.at[pl.ds(0, 8)],
        EARLY: wbuf.at[pl.ds(0, 5)], LATE: er.at[0],
    }

    barrier = pltpu.get_barrier_semaphore()
    for g in NEIGHBOURS:
        pl.semaphore_signal(barrier, inc=1, device_id=device(g, 1), device_id_type=MESH)

    small = [
        pltpu.make_async_copy(src, dst, lsem.at[n])
        for n, (src, dst) in enumerate((
            (oc_hbm, oc), (vel_hbm, fields.at[pl.ds(0, 2)]), (mask_hbm, maskbuf),
            (atm_hbm.at[:, pl.ds(0, 8), :], abuf), (mix_hbm, mbuf), (inter_hbm, inter),
        ))
    ]
    weights = pltpu.make_async_copy(w_hbm, wbuf, wsem)
    columns = pltpu.make_async_copy(atm_hbm, xbuf, xsem)
    small[5].start()
    small[3].start()
    weights.start()

    small[5].wait()
    for e in range(SLOTS):
        req[e // CAP, pl.ds(e % CAP, 1), :] = jnp.full((1, BLK), inter[1, e], jnp.int32)
    reqs[4] = req[4]

    small[3].wait()
    for b in range(ACB):
        block = abuf[:, 0, b * BLK:(b + 1) * BLK]
        hi, lo = split2(block)
        ast[b, 0:K, :] = hi
        ast[b, K:2 * K, :] = lo
    for load in small[0:3] + small[4:5]:
        load.start()
    weights.wait()
    columns.start()

    def contrib_rows(g):
        for s in range(CAP):
            e = g * CAP + s
            hi, lo = split2(wbuf[jnp.maximum(inter[2, e], 0)])
            a = ast[jnp.maximum(inter[0, e], 0)]
            first = dot_nt(a, hi)
            second = dot_nt(a[0:K], lo)
            cbuf[g, pl.ds(s, K, stride=CAP), :] = first[0:K] + first[K:2 * K] + second

    contrib_rows(NEIGHBOURS[0])
    pl.semaphore_wait(barrier, len(NEIGHBOURS))

    requests = [message(REQUEST, g, req.at[g], reqs.at[g]) for g in NEIGHBOURS]
    for copy in requests:
        copy.start()

    message(CONTRIB, NEIGHBOURS[0], cbuf.at[NEIGHBOURS[0]], cin.at[NEIGHBOURS[0]]).start()

    def contrib_group(t, carry):
        g = (t // 2) * (1 - t % 2) + (8 - t // 2) * (t % 2)
        contrib_rows(g)

        @pl.when(g != 4)
        def _():
            message(CONTRIB, g, cbuf.at[g], cin.at[g]).start()

        return carry

    lax.fori_loop(1, 9, contrib_group, 0)
    cin[4] = cbuf[4]

    for load in small[0:3]:
        load.wait()
    wet = maskbuf[...].astype(F32)
    fields[2] = wet
    vel = fields

    er[:, NQ * 48 + 8:EARLY_ROWS, :] = jnp.zeros((2, 8, BLK), F32)
    es[:, 72:EARLY_STRIP, :] = jnp.zeros((2, EARLY_STRIP - 72, BLK), F32)
    lane = lax.broadcasted_iota(jnp.int32, (8, BLK), 1)
    for q in range(NQ):
        for lev in range(1, OL):
            for p in range(4):
                row = q * 48 + (lev - 1) * 16 + p * 4
                er[0, row:row + HW, :] = oc[4 * q + p, lev, 0:HW, :]
                er[1, row:row + HW, :] = oc[4 * q + p, lev, OY - HW:OY, :]
    for n in range(3):
        row = NQ * 48 + n * 4
        field = vel[n] if n < 2 else wet
        er[0, row:row + HW, :] = field[0:HW]
        er[1, row:row + HW, :] = field[OY - HW:OY]
    groups = [
        (t * 3 + lev - 1, turned([oc[k, lev] for k in range(3 * t, min(3 * t + 3, K))]))
        for t in range(TRIPLES) for lev in range(1, OL)
    ]
    cut_edges(groups + [(EARLY_GROUPS, turned([vel[0], vel[1], wet]))], es, ec, lane)

    sides = {1: 0, 7: 1}
    ends = {3: 0, 5: 1}
    corners = {0: 0, 2: 1, 6: 2, 8: 3}

    def halo(kind, rows, corner, strip, rows_in, corner_in, strip_in, count):
        copies = []
        for g in NEIGHBOURS:
            if g in sides:
                n = sides[g]
                copies.append(message(kind, g, rows.at[n, pl.ds(0, count)], rows_in.at[n]))
            elif g in ends:
                n = ends[g]
                copies.append(message(kind, g, strip.at[n], strip_in.at[n]))
            else:
                n = corners[g]
                copies.append(message(kind, g, corner.at[n], corner_in.at[n]))
        return copies

    early = halo(EARLY, er, ec, es, er_in, ec_in, es_in, EARLY_ROWS)
    for copy in early:
        copy.start()

    all_of(REQUEST, rsem, spans[REQUEST])
    lanes = lax.broadcasted_iota(jnp.int32, (SLOTS, BLK), 1)
    chosen = (reqs[...].reshape(SLOTS, BLK) == lanes).astype(F32)
    pick = chosen[:, 0:OY].astype(BF16)
    for k in range(0, K, 2):
        pair = jnp.concatenate([oc[k, 0] * wet, oc[k + 1, 0] * wet], 1)
        hi, mid, lo = split3(pair)
        rows = dot(pick, hi) + dot(pick, mid) + dot(pick, lo)
        for g in range(9):
            sbuf[g, k * CAP:(k + 1) * CAP, :] = rows[g * CAP:(g + 1) * CAP, 0:BLK]
            sbuf[g, (k + 1) * CAP:(k + 2) * CAP, :] = rows[g * CAP:(g + 1) * CAP, BLK:2 * BLK]
    rows = dot(pick, wet.astype(BF16))
    for g in range(9):
        sbuf[g, K * CAP:(K + 1) * CAP, :] = rows[g * CAP:(g + 1) * CAP]
    sin[4] = sbuf[4]
    for g in NEIGHBOURS:
        message(SURFACE, g, sbuf.at[g], sin.at[g], -1).start()

    small[4].wait()
    for b in range(ACB):
        m = jnp.concatenate([mbuf[b], jnp.zeros((LA, 2 * BLK - LA), F32)], 1)
        first_column[b] = jnp.broadcast_to(m[:, 0:1], (LA, BLK))
        mh = m.astype(BF16).astype(F32)
        stacked[b] = (mh + pltpu.roll(mh, 80, 1) + pltpu.roll(m - mh, 160, 1)).astype(BF16)
    upper = lax.broadcasted_iota(jnp.int32, (8, BLK), 0) > 0

    columns.wait()

    def mixing(c, carry):
        for b in range(ACB):
            cols = slice(b * BLK, (b + 1) * BLK)
            sides = []
            for n in range(2):
                x = jnp.concatenate([
                    jnp.where(upper, xbuf[2 * c + n, 0:8, cols], 0.0),
                    xbuf[2 * c + n, 8:LA, cols],
                    jnp.zeros((8, BLK), F32),
                ], 0)
                hi, lo = split2(x)
                sides.append(jnp.concatenate([hi, lo, hi, jnp.zeros((16, BLK), BF16)], 0))
            out = dot(stacked[b], jnp.concatenate(sides, 1))
            mixed[2 * c, :, cols] = out[:, 0:BLK]
            mixed[2 * c + 1, :, cols] = out[:, BLK:2 * BLK]
        return carry

    lax.fori_loop(0, 8, mixing, 0)

    place = chosen.T[0:OY].astype(BF16)
    all_of(CONTRIB, rsem, spans[CONTRIB])
    for k in range(0, K, 2):
        pair = jnp.concatenate(
            [cin[:, n * CAP:(n + 1) * CAP, :].reshape(SLOTS, BLK) for n in (k, k + 1)], 1
        )
        hi, mid, lo = split3(pair)
        arrived = dot(place, hi) + dot(place, mid) + dot(place, lo)
        for n in range(2):
            old = oc[k + n, 0]
            new = old + ocean_uptake * wet * (arrived[:, n * BLK:(n + 1) * BLK] - old)
            oc[k + n, 0] = new
            lr[0, (k + n) * 4:(k + n) * 4 + 4, :] = new[0:HW]
            lr[1, (k + n) * 4:(k + n) * 4 + 4, :] = new[OY - HW:OY]
    groups = [
        (t, turned([oc[k, 0] for k in range(3 * t, min(3 * t + 3, K))])) for t in range(TRIPLES)
    ]
    cut_edges(groups, ls, lc, lane)
    late = halo(LATE, lr, lc, ls, lr_in, lc_in, ls_in, 4 * K)
    for copy in late:
        copy.start()


    all_of(EARLY, rsem, spans[EARLY])
    set_coefficients(coef, fields, er_in, outer_columns(es_in, ec_in, EARLY_GROUPS, lane), lane)
    for t in range(TRIPLES):
        ks = range(3 * t, min(3 * t + 3, K))
        for lev in range(1, OL):
            rows = [(k // 4) * 48 + (lev - 1) * 16 + (k % 4) * HW for k in ks]
            norths, souths = ([er_in[side, row:row + HW, :] for row in rows] for side in range(2))
            store_tile(
                state, coef, t, lev, widen([oc[k, lev] for k in ks], norths, souths),
                outer_columns(es_in, ec_in, t * 3 + lev - 1, lane),
            )

    acc[...] = jnp.zeros_like(acc)

    def return_group(t, carry):
        near = (8 - t) // 6
        u = (t + 6) % 9
        g = near * (3 + t) + (1 - near) * ((u // 2) * (1 - u % 2) + (8 - u // 2) * (u % 2))

        @pl.when(g != 4)
        def _():
            message(SURFACE, g, sbuf.at[g], sin.at[g], -1).wait_recv()

        parts = []
        for s in range(CAP):
            e = g * CAP + s
            hi, lo = split2(wbuf[jnp.maximum(inter[2, e], 0)])
            ahi, alo = split2(sin[g, pl.ds(s, K, stride=CAP), :])
            wets = jnp.broadcast_to(sin[g, pl.ds(K * CAP + s, 1), :], (K, BLK)).astype(BF16)
            lhs = jnp.concatenate([ahi, alo, wets], 0)
            first = dot(lhs, hi)
            second = dot(lhs, lo)
            parts.append((
                first[0:K] + first[K:2 * K] + second[0:K],
                first[2 * K:2 * K + 8] + second[2 * K:2 * K + 8],
            ))
        for b in range(ACB):
            tracers, wets = acc[b, 0:K, :], acc[b, K:K + 8, :]
            for s in range(CAP):
                e = g * CAP + s
                here = jnp.where((inter[0, e] == b) & (inter[1, e] >= 0), 1.0, 0.0).astype(F32)
                tracers = tracers + here * parts[s][0]
                wets = wets + here * parts[s][1]
            acc[b, 0:K, :] = tracers
            acc[b, K:K + 8, :] = wets
        return carry

    lax.fori_loop(0, 7, return_group, 0)

    all_of(LATE, rsem, spans[LATE])
    for t in range(TRIPLES):
        ks = range(3 * t, min(3 * t + 3, K))
        norths, souths = ([lr_in[side, k * HW:(k + 1) * HW, :] for k in ks] for side in range(2))
        store_tile(
            state, coef, t, 0, widen([oc[k, 0] for k in ks], norths, souths),
            outer_columns(ls_in, lc_in, t, lane),
        )

    lax.fori_loop(7, 9, return_group, 0)
    for b in range(ACB):
        old = abuf[:, 0, b * BLK:(b + 1) * BLK]
        bottom[pl.ds(b, K, stride=ACB), :] = old + air_uptake * (
            acc[b, 0:K, :] - acc[b, K:K + 1, :] * old
        )

    for kind in range(5):
        all_of(kind, ssem, spans[kind])


def exchange(inter, atm, mix, oc, vel, mask, weights):
    vmem = pl.BlockSpec(memory_space=pltpu.VMEM)
    hbm = pl.BlockSpec(memory_space=pltpu.HBM)
    shapes = [
        (K, LA, ACB * BLK), (ACB, LA, BLK), (K * ACB, BLK),
        (7, COLS, BLK), (TRIPLES, OL, PADDED, BLK),
    ]
    halos = [
        (2, EARLY_ROWS, BLK), (4, 8, BLK), (2, EARLY_STRIP, BLK),
        (2, 4 * K, BLK), (4, 8, BLK), (2, LATE_STRIP, BLK),
    ]
    return pl.pallas_call(
        exchange_kernel,
        out_shape=[jax.ShapeDtypeStruct(s, F32) for s in shapes],
        in_specs=[hbm] * 7,
        out_specs=[vmem] * len(shapes),
        scratch_shapes=[
            pltpu.SMEM((3, SLOTS), jnp.int32),
            pltpu.VMEM((K, OL, OY, BLK), F32),
            pltpu.VMEM((3, OY, BLK), F32),
            pltpu.VMEM((WSL, BLK, BLK), F32),
            pltpu.VMEM((K, 8, ACB * BLK), F32),
            pltpu.VMEM((K, LA, ACB * BLK), F32),
            pltpu.VMEM((ACB, LA, LA), F32),
            pltpu.VMEM((OY, BLK), jnp.int32),
            pltpu.VMEM((ACB, LA, 2 * BLK), BF16),
            pltpu.VMEM((ACB, 2 * K, BLK), BF16),
            pltpu.VMEM((9, CAP, BLK), jnp.int32),
            pltpu.VMEM((9, CAP, BLK), jnp.int32),
            pltpu.VMEM((9, K * CAP, BLK), F32),
            pltpu.VMEM((9, K * CAP, BLK), F32),
            pltpu.VMEM((9, (K + 1) * CAP, BLK), F32),
            pltpu.VMEM((9, (K + 1) * CAP, BLK), F32),
            pltpu.VMEM((ACB, K + 8, BLK), F32),
            *[pltpu.VMEM(shape, F32) for shape in halos * 2],
            pltpu.SemaphoreType.DMA,
            pltpu.SemaphoreType.DMA,
            pltpu.SemaphoreType.DMA((6,)),
            pltpu.SemaphoreType.DMA((5,)),
            pltpu.SemaphoreType.DMA((5,)),
            pltpu.SemaphoreType.DMA((9,)),
        ],
        compiler_params=pltpu.CompilerParams(
            collective_id=0, has_side_effects=True, vmem_limit_bytes=30 * 2**20
        ),
        name="exchange",
    )(*(
        pltpu.with_memory_space_constraint(x, pltpu.HBM)
        for x in (inter, atm, mix, oc, vel, mask, weights)
    ))


def step_kernel(
    mixed, first_column, bottom, coef, state,
    atm_out, oc_out, atm_stage, oc_stage, work, shift, asem, osem,
):
    row = lax.broadcasted_iota(jnp.int32, (2 * BLK, 2 * BLK), 0) % BLK
    col = lax.broadcasted_iota(jnp.int32, (2 * BLK, 2 * BLK), 1)
    step = jnp.where(col < BLK, 1, BLK - 1)
    shift[...] = (row == (col + step) % BLK).astype(F32).astype(BF16)

    def ocean(t, carry):
        for n in range(3):
            k = jnp.minimum(3 * t + n, K - 1)
            surface = bottom[pl.ds(pl.multiple_of(k * ACB, ACB), ACB), :]
            for b in range(ACB):
                cols = slice(b * BLK, (b + 1) * BLK)
                atm_stage[3 * t + n, :, cols] = (
                    mixed[k, :, cols] + first_column[b] * surface[b:b + 1]
                )
        for sub in range(NSUB):
            def source(lev, start):
                if sub == 0:
                    return state[t, lev, start:start + 8, :]
                return work[(sub - 1) % 2, lev, start:start + 8, :]

            bottom_level = OL - 1
            whole = jnp.concatenate(
                [source(bottom_level, 8 + tile * 8) for tile in range(COLS // 8 + 1)], 0
            )
            moved = dot(jnp.concatenate(split2(whole), 1), shift[...])

            for tile, levels in (
                [(tile, range(bottom_level)) for tile in range(COLS // 8)]
                + [(tile, [bottom_level]) for tile in range(COLS // 8)]
            ):
                start = 8 + tile * 8
                c = [coef[n, tile * 8:tile * 8 + 8, :] for n in range(6)]
                x = {
                    lev: source(lev, start)
                    for lev in range(max(levels[0] - 1, 0), min(levels[-1] + 2, OL))
                }
                for lev in levels:
                    if lev == bottom_level:
                        north = moved[tile * 8:tile * 8 + 8, 0:BLK]
                        south = moved[tile * 8:tile * 8 + 8, BLK:2 * BLK]
                    else:
                        north = pltpu.roll(x[lev], BLK - 1, 1)
                        south = pltpu.roll(x[lev], 1, 1)
                    new = (
                        c[0] * source(lev, start + 1)
                        + c[1] * source(lev, start - 1)
                        + c[2] * north
                        + c[3] * south
                        + c[4] * (x[max(lev - 1, 0)] + x[min(lev + 1, OL - 1)])
                        + c[5] * x[lev]
                    )
                    work[sub % 2, lev, start:start + 8, :] = new
                    if tile == 0:
                        work[sub % 2, lev, 8 + COLS:PADDED, :] = new
                    if tile == COLS // 8 - 1:
                        work[sub % 2, lev, 0:8, :] = new
        for lev in range(OL):
            out = work[(NSUB - 1) % 2, lev, 8:8 + BLK, :].T
            for n in range(3):
                oc_stage[3 * t + n, lev] = out[n * LANES:n * LANES + OY]

        @pl.when(t < TRIPLES - 1)
        def _():
            three = pl.ds(3 * t, 3)
            pltpu.make_async_copy(atm_stage.at[three], atm_out.at[three], asem.at[t]).start()
            pltpu.make_async_copy(oc_stage.at[three], oc_out.at[three], osem.at[t]).start()

        return carry

    lax.fori_loop(0, TRIPLES, ocean, 0)
    copies = [
        pltpu.make_async_copy(stage.at[part], out.at[part], sem.at[TRIPLES - 1])
        for part in [pl.ds(K - 1, 1)]
        for stage, out, sem in ((atm_stage, atm_out, asem), (oc_stage, oc_out, osem))
    ]
    for copy in copies:
        copy.start()
    for t in range(TRIPLES - 1):
        three = pl.ds(3 * t, 3)
        pltpu.make_async_copy(atm_stage.at[three], atm_out.at[three], asem.at[t]).wait()
        pltpu.make_async_copy(oc_stage.at[three], oc_out.at[three], osem.at[t]).wait()
    for copy in copies:
        copy.wait()


def local_step(arrays):
    vmem = pl.BlockSpec(memory_space=pltpu.VMEM)
    hbm = pl.BlockSpec(memory_space=pltpu.HBM)
    return pl.pallas_call(
        step_kernel,
        out_shape=[
            jax.ShapeDtypeStruct((K, LA, ACB * BLK), F32),
            jax.ShapeDtypeStruct((K, OL, OY, BLK), F32),
        ],
        in_specs=[vmem] * len(arrays),
        out_specs=[hbm, hbm],
        scratch_shapes=[
            pltpu.VMEM((3 * TRIPLES, LA, ACB * BLK), F32),
            pltpu.VMEM((3 * TRIPLES, OL, OY, BLK), F32),
            pltpu.VMEM((2, OL, PADDED, BLK), F32),
            pltpu.VMEM((2 * BLK, 2 * BLK), BF16),
            pltpu.SemaphoreType.DMA((TRIPLES,)),
            pltpu.SemaphoreType.DMA((TRIPLES,)),
        ],
        compiler_params=pltpu.CompilerParams(vmem_limit_bytes=20 * 2**20),
        name="step",
    )(*arrays)


def body(atm, mix, oc, vel, mask, inter, weights):
    return tuple(local_step(exchange(inter, atm, mix, oc, vel, mask, weights)))


def solution(mesh):
    in_specs = (
        P(None, None, ("gx", "gy")),
        P(("gx", "gy"), None, None),
        P(None, None, "gy", "gx"),
        P(None, "gy", "gx"),
        P("gy", "gx"),
        P(None, ("gx", "gy")),
        P(("gx", "gy"), None, None),
    )
    out_specs = (P(None, None, ("gx", "gy")), P(None, None, "gy", "gx"))
    return jax.shard_map(body, mesh=mesh, in_specs=in_specs, out_specs=out_specs, check_vma=False)
```

```python
import functools

import jax
import jax.numpy as jnp
from jax import lax
from jax.experimental import pallas as pl
from jax.experimental.pallas import tpu as pltpu
from jax.sharding import PartitionSpec as P

K = 16
LA = 72
OL = 4
OY = 32
BLK = 128
ACB = 8
CAP = 8
WSL = 64
NSUB = 4
SLOTS = 9 * CAP
HW = NSUB
LANES = OY + 2 * HW
TRIPLES = 6
EARLY_GROUPS = TRIPLES * (OL - 1)
COLS = BLK + 2 * HW
PADDED = COLS + 16

ocean_uptake = 0.5
air_uptake = 0.5
mix_horizontal = 0.15
mix_vertical = 0.2

F32 = jnp.float32
BF16 = jnp.bfloat16
MESH = pl.DeviceIdType.MESH
NEIGHBOURS = (0, 8, 1, 7, 2, 6, 3, 5)
REQUEST, CONTRIB, SURFACE, EARLY, LATE = range(5)
NQ = 4
EARLY_ROWS = NQ * 48 + 16
EARLY_STRIP = 96
LATE_STRIP = 24


def split2(x):
    hi = x.astype(BF16)
    return hi, (x - hi.astype(F32)).astype(BF16)


def split3(x):
    hi = x.astype(BF16)
    rest = x - hi.astype(F32)
    mid = rest.astype(BF16)
    return hi, mid, (rest - mid.astype(F32)).astype(BF16)


def dot(a, b):
    return jnp.dot(a, b, preferred_element_type=F32)


def dot_nt(a, b):
    return lax.dot_general(a, b, (((1,), (1,)), ((), ())), preferred_element_type=F32)


def turned(tiles):
    gap = jnp.zeros((2 * HW, BLK), F32)
    rows = []
    for tile in tiles:
        rows += [tile, gap]
    full = jnp.concatenate(rows, 0)
    if full.shape[0] < BLK:
        full = jnp.concatenate([full, jnp.zeros((BLK - full.shape[0], BLK), F32)], 0)
    return full.T


def cut_edges(groups, strips, ends, lane):
    blocks = {}
    for n, full in groups:
        strips[0, n * HW:(n + 1) * HW, :] = full[0:HW]
        strips[1, n * HW:(n + 1) * HW, :] = full[BLK - HW:BLK]
        edge = jnp.concatenate([full[0:HW], full[BLK - HW:BLK]], 0)
        here = (lane % LANES) // HW == n % 10
        low = pltpu.roll(edge, (n % 10) * HW, 1)
        high = pltpu.roll(edge, ((n % 10) * HW - (OY - HW)) % BLK, 1)
        old = blocks.get(n // 10, (jnp.zeros((8, BLK), F32),) * 2)
        blocks[n // 10] = (jnp.where(here, low, old[0]), jnp.where(here, high, old[1]))
    for b in range(2):
        low, high = blocks.get(b, (jnp.zeros((8, BLK), F32),) * 2)
        rows = slice(b * HW, (b + 1) * HW)
        ends[0, rows, :] = low[0:HW]
        ends[1, rows, :] = low[HW:8]
        ends[2, rows, :] = high[0:HW]
        ends[3, rows, :] = high[HW:8]


def widen(tiles, norths, souths):
    gap = jnp.zeros((HW, BLK), F32)
    rows = []
    for n in range(3):
        n_row = norths[n] if n < len(tiles) else gap
        s_row = souths[n + 1] if n + 1 < len(tiles) else gap
        rows += [tiles[n] if n < len(tiles) else jnp.zeros((OY, BLK), F32), n_row, s_row]
    return jnp.concatenate(rows + [gap, souths[0]], 0).T


def outer_columns(strips, ends, n, lane):
    shifted = (lane + HW) % BLK
    north = (shifted % LANES >= OY + HW) & (shifted < 3 * LANES)
    south = (shifted % LANES < HW) & (shifted < 3 * LANES)
    rows = slice((n // 10) * HW, (n // 10 + 1) * HW)
    mine = jnp.concatenate(
        [strips[0, n * HW:(n + 1) * HW, :], strips[1, n * HW:(n + 1) * HW, :]], 0
    )
    above = jnp.concatenate([ends[0, rows, :], ends[1, rows, :]], 0)
    below = jnp.concatenate([ends[2, rows, :], ends[3, rows, :]], 0)
    above = pltpu.roll(above, (OY - (n % 10) * HW) % BLK, 1)
    below = pltpu.roll(below, (BLK - HW - (n % 10) * HW) % BLK, 1)
    return jnp.where(north, above, jnp.where(south, below, mine))


def store_tile(state, coef, t, lev, inner, outer):
    inner = inner * coef[6, 0:BLK, :]
    outer = outer * coef[6, BLK:COLS, :]
    state[t, lev, 0:8, :] = outer
    state[t, lev, 8:8 + BLK, :] = inner
    state[t, lev, 8 + BLK:8 + COLS, :] = outer
    state[t, lev, 8 + COLS:PADDED, :] = inner[0:8]


def set_coefficients(coef, own, er, ends, lane):
    shifted = (lane + HW) % BLK
    fields = []
    for n in range(3):
        row = NQ * 48 + n * HW
        inner = widen([own[n]] * 3, [er[0, row:row + HW, :]] * 3, [er[1, row:row + HW, :]] * 3)
        parts = [pltpu.roll(ends, ((m - n) * LANES) % BLK, 1) for m in range(3)]
        outer = jnp.where(
            shifted < LANES, parts[0], jnp.where(shifted < 2 * LANES, parts[1], parts[2])
        )
        fields.append(jnp.concatenate([inner, outer], 0))
    u, v, wet = fields
    coef[0] = wet * (mix_horizontal - 0.5 * u)
    coef[1] = wet * (mix_horizontal + 0.5 * u)
    coef[2] = wet * (mix_horizontal - 0.5 * v)
    coef[3] = wet * (mix_horizontal + 0.5 * v)
    coef[4] = wet * mix_vertical
    coef[5] = wet * (1.0 - 4.0 * mix_horizontal - 2.0 * mix_vertical)
    coef[6] = wet


def exchange_kernel(
    inter_hbm, atm_hbm, mix_hbm, oc_hbm, vel_hbm, mask_hbm, w_hbm,
    mixed, first_column, bottom, coef, state,
    inter, oc, fields, wbuf, abuf, xbuf, mbuf, maskbuf, stacked, ast,
    req, reqs, cbuf, cin, sbuf, sin, acc,
    er, ec, es, lr, lc, ls, er_in, ec_in, es_in, lr_in, lc_in, ls_in,
    wsem, xsem, lsem, ssem, rsem, surf_sem,
):
    nx, ny = lax.axis_size("gx"), lax.axis_size("gy")
    i, j = lax.axis_index("gx"), lax.axis_index("gy")

    def device(g, sign):
        dy, dx = g // 3 - 1, g % 3 - 1
        return ((i + sign * dx + nx) % nx, (j + sign * dy + ny) % ny)

    def message(kind, g, src, dst, sign=1):
        return pltpu.make_async_remote_copy(
            src_ref=src, dst_ref=dst, send_sem=ssem.at[kind],
            recv_sem=surf_sem.at[g] if kind == SURFACE else rsem.at[kind],
            device_id=device(g, sign), device_id_type=MESH,
        )

    def all_of(kind, sem, span):
        pltpu.make_async_copy(span, span, sem.at[kind]).wait()

    spans = {
        REQUEST: req.at[pl.ds(0, 8)], CONTRIB: cbuf.at[pl.ds(0, 8)], SURFACE: sbuf.at[pl.ds(0, 8)],
        EARLY: wbuf.at[pl.ds(0, 5)], LATE: er.at[0],
    }

    barrier = pltpu.get_barrier_semaphore()
    for g in NEIGHBOURS:
        pl.semaphore_signal(barrier, inc=1, device_id=device(g, 1), device_id_type=MESH)

    small = [
        pltpu.make_async_copy(src, dst, lsem.at[n])
        for n, (src, dst) in enumerate((
            (oc_hbm, oc), (vel_hbm, fields.at[pl.ds(0, 2)]), (mask_hbm, maskbuf),
            (atm_hbm.at[:, pl.ds(0, 8), :], abuf), (mix_hbm, mbuf), (inter_hbm, inter),
        ))
    ]
    weights = pltpu.make_async_copy(w_hbm, wbuf, wsem)
    columns = pltpu.make_async_copy(atm_hbm, xbuf, xsem)
    small[5].start()
    small[3].start()
    weights.start()

    small[5].wait()
    for e in range(SLOTS):
        req[e // CAP, pl.ds(e % CAP, 1), :] = jnp.full((1, BLK), inter[1, e], jnp.int32)
    reqs[4] = req[4]

    small[3].wait()
    for b in range(ACB):
        block = abuf[:, 0, b * BLK:(b + 1) * BLK]
        hi, lo = split2(block)
        ast[b, 0:K, :] = hi
        ast[b, K:2 * K, :] = lo
    for load in small[0:3] + small[4:5]:
        load.start()
    weights.wait()
    columns.start()

    def contrib_rows(g):
        for s in range(CAP):
            e = g * CAP + s
            hi, lo = split2(wbuf[jnp.maximum(inter[2, e], 0)])
            a = ast[jnp.maximum(inter[0, e], 0)]
            first = dot_nt(a, hi)
            second = dot_nt(a[0:K], lo)
            cbuf[g, pl.ds(s, K, stride=CAP), :] = first[0:K] + first[K:2 * K] + second

    contrib_rows(NEIGHBOURS[0])
    pl.semaphore_wait(barrier, len(NEIGHBOURS))

    requests = [message(REQUEST, g, req.at[g], reqs.at[g]) for g in NEIGHBOURS]
    for copy in requests:
        copy.start()

    message(CONTRIB, NEIGHBOURS[0], cbuf.at[NEIGHBOURS[0]], cin.at[NEIGHBOURS[0]]).start()

    def contrib_group(t, carry):
        g = (t // 2) * (1 - t % 2) + (8 - t // 2) * (t % 2)
        contrib_rows(g)

        @pl.when(g != 4)
        def _():
            message(CONTRIB, g, cbuf.at[g], cin.at[g]).start()

        return carry

    lax.fori_loop(1, 9, contrib_group, 0)
    cin[4] = cbuf[4]

    for load in small[0:3]:
        load.wait()
    wet = maskbuf[...].astype(F32)
    fields[2] = wet
    vel = fields

    er[:, NQ * 48 + 8:EARLY_ROWS, :] = jnp.zeros((2, 8, BLK), F32)
    es[:, 72:EARLY_STRIP, :] = jnp.zeros((2, EARLY_STRIP - 72, BLK), F32)
    lane = lax.broadcasted_iota(jnp.int32, (8, BLK), 1)
    for q in range(NQ):
        for lev in range(1, OL):
            for p in range(4):
                row = q * 48 + (lev - 1) * 16 + p * 4
                er[0, row:row + HW, :] = oc[4 * q + p, lev, 0:HW, :]
                er[1, row:row + HW, :] = oc[4 * q + p, lev, OY - HW:OY, :]
    for n in range(3):
        row = NQ * 48 + n * 4
        field = vel[n] if n < 2 else wet
        er[0, row:row + HW, :] = field[0:HW]
        er[1, row:row + HW, :] = field[OY - HW:OY]
    groups = [
        (t * 3 + lev - 1, turned([oc[k, lev] for k in range(3 * t, min(3 * t + 3, K))]))
        for t in range(TRIPLES) for lev in range(1, OL)
    ]
    cut_edges(groups + [(EARLY_GROUPS, turned([vel[0], vel[1], wet]))], es, ec, lane)

    sides = {1: 0, 7: 1}
    ends = {3: 0, 5: 1}
    corners = {0: 0, 2: 1, 6: 2, 8: 3}

    def halo(kind, rows, corner, strip, rows_in, corner_in, strip_in, count):
        copies = []
        for g in NEIGHBOURS:
            if g in sides:
                n = sides[g]
                copies.append(message(kind, g, rows.at[n, pl.ds(0, count)], rows_in.at[n]))
            elif g in ends:
                n = ends[g]
                copies.append(message(kind, g, strip.at[n], strip_in.at[n]))
            else:
                n = corners[g]
                copies.append(message(kind, g, corner.at[n], corner_in.at[n]))
        return copies

    early = halo(EARLY, er, ec, es, er_in, ec_in, es_in, EARLY_ROWS)
    for copy in early:
        copy.start()

    all_of(REQUEST, rsem, spans[REQUEST])
    lanes = lax.broadcasted_iota(jnp.int32, (SLOTS, BLK), 1)
    chosen = (reqs[...].reshape(SLOTS, BLK) == lanes).astype(F32)
    pick = chosen[:, 0:OY].astype(BF16)
    for k in range(0, K, 2):
        pair = jnp.concatenate([oc[k, 0] * wet, oc[k + 1, 0] * wet], 1)
        hi, mid, lo = split3(pair)
        rows = dot(pick, hi) + dot(pick, mid) + dot(pick, lo)
        for g in range(9):
            sbuf[g, k * CAP:(k + 1) * CAP, :] = rows[g * CAP:(g + 1) * CAP, 0:BLK]
            sbuf[g, (k + 1) * CAP:(k + 2) * CAP, :] = rows[g * CAP:(g + 1) * CAP, BLK:2 * BLK]
    rows = dot(pick, wet.astype(BF16))
    for g in range(9):
        sbuf[g, K * CAP:(K + 1) * CAP, :] = rows[g * CAP:(g + 1) * CAP]
    sin[4] = sbuf[4]
    for g in NEIGHBOURS:
        message(SURFACE, g, sbuf.at[g], sin.at[g], -1).start()

    small[4].wait()
    for b in range(ACB):
        m = jnp.concatenate([mbuf[b], jnp.zeros((LA, 2 * BLK - LA), F32)], 1)
        first_column[b] = jnp.broadcast_to(m[:, 0:1], (LA, BLK))
        mh = m.astype(BF16).astype(F32)
        stacked[b] = (mh + pltpu.roll(mh, 80, 1) + pltpu.roll(m - mh, 160, 1)).astype(BF16)
    upper = lax.broadcasted_iota(jnp.int32, (8, BLK), 0) > 0

    columns.wait()

    def mixing(c, carry):
        for b in range(ACB):
            cols = slice(b * BLK, (b + 1) * BLK)
            sides = []
            for n in range(2):
                x = jnp.concatenate([
                    jnp.where(upper, xbuf[2 * c + n, 0:8, cols], 0.0),
                    xbuf[2 * c + n, 8:LA, cols],
                    jnp.zeros((8, BLK), F32),
                ], 0)
                hi, lo = split2(x)
                sides.append(jnp.concatenate([hi, lo, hi, jnp.zeros((16, BLK), BF16)], 0))
            out = dot(stacked[b], jnp.concatenate(sides, 1))
            mixed[2 * c, :, cols] = out[:, 0:BLK]
            mixed[2 * c + 1, :, cols] = out[:, BLK:2 * BLK]
        return carry

    lax.fori_loop(0, 8, mixing, 0)

    place = chosen.T[0:OY].astype(BF16)
    all_of(CONTRIB, rsem, spans[CONTRIB])
    for k in range(0, K, 2):
        pair = jnp.concatenate(
            [cin[:, n * CAP:(n + 1) * CAP, :].reshape(SLOTS, BLK) for n in (k, k + 1)], 1
        )
        hi, mid, lo = split3(pair)
        arrived = dot(place, hi) + dot(place, mid) + dot(place, lo)
        for n in range(2):
            old = oc[k + n, 0]
            new = old + ocean_uptake * wet * (arrived[:, n * BLK:(n + 1) * BLK] - old)
            oc[k + n, 0] = new
            lr[0, (k + n) * 4:(k + n) * 4 + 4, :] = new[0:HW]
            lr[1, (k + n) * 4:(k + n) * 4 + 4, :] = new[OY - HW:OY]
    groups = [
        (t, turned([oc[k, 0] for k in range(3 * t, min(3 * t + 3, K))])) for t in range(TRIPLES)
    ]
    cut_edges(groups, ls, lc, lane)
    late = halo(LATE, lr, lc, ls, lr_in, lc_in, ls_in, 4 * K)
    for copy in late:
        copy.start()


    all_of(EARLY, rsem, spans[EARLY])
    set_coefficients(coef, fields, er_in, outer_columns(es_in, ec_in, EARLY_GROUPS, lane), lane)
    for t in range(TRIPLES):
        ks = range(3 * t, min(3 * t + 3, K))
        for lev in range(1, OL):
            rows = [(k // 4) * 48 + (lev - 1) * 16 + (k % 4) * HW for k in ks]
            norths, souths = ([er_in[side, row:row + HW, :] for row in rows] for side in range(2))
            store_tile(
                state, coef, t, lev, widen([oc[k, lev] for k in ks], norths, souths),
                outer_columns(es_in, ec_in, t * 3 + lev - 1, lane),
            )

    acc[...] = jnp.zeros_like(acc)

    def return_group(t, carry):
        near = (8 - t) // 6
        u = (t + 6) % 9
        g = near * (3 + t) + (1 - near) * ((u // 2) * (1 - u % 2) + (8 - u // 2) * (u % 2))

        @pl.when(g != 4)
        def _():
            message(SURFACE, g, sbuf.at[g], sin.at[g], -1).wait_recv()

        parts = []
        for s in range(CAP):
            e = g * CAP + s
            hi, lo = split2(wbuf[jnp.maximum(inter[2, e], 0)])
            ahi, alo = split2(sin[g, pl.ds(s, K, stride=CAP), :])
            wets = jnp.broadcast_to(sin[g, pl.ds(K * CAP + s, 1), :], (K, BLK)).astype(BF16)
            lhs = jnp.concatenate([ahi, alo, wets], 0)
            first = dot(lhs, hi)
            second = dot(lhs, lo)
            parts.append((
                first[0:K] + first[K:2 * K] + second[0:K],
                first[2 * K:2 * K + 8] + second[2 * K:2 * K + 8],
            ))
        for b in range(ACB):
            tracers, wets = acc[b, 0:K, :], acc[b, K:K + 8, :]
            for s in range(CAP):
                e = g * CAP + s
                here = jnp.where((inter[0, e] == b) & (inter[1, e] >= 0), 1.0, 0.0).astype(F32)
                tracers = tracers + here * parts[s][0]
                wets = wets + here * parts[s][1]
            acc[b, 0:K, :] = tracers
            acc[b, K:K + 8, :] = wets
        return carry

    lax.fori_loop(0, 9, return_group, 0)
    for b in range(ACB):
        old = abuf[:, 0, b * BLK:(b + 1) * BLK]
        bottom[pl.ds(b, K, stride=ACB), :] = old + air_uptake * (
            acc[b, 0:K, :] - acc[b, K:K + 1, :] * old
        )

    all_of(LATE, rsem, spans[LATE])
    for t in range(TRIPLES):
        ks = range(3 * t, min(3 * t + 3, K))
        norths, souths = ([lr_in[side, k * HW:(k + 1) * HW, :] for k in ks] for side in range(2))
        store_tile(
            state, coef, t, 0, widen([oc[k, 0] for k in ks], norths, souths),
            outer_columns(ls_in, lc_in, t, lane),
        )

    for kind in range(5):
        all_of(kind, ssem, spans[kind])


def exchange(inter, atm, mix, oc, vel, mask, weights):
    vmem = pl.BlockSpec(memory_space=pltpu.VMEM)
    hbm = pl.BlockSpec(memory_space=pltpu.HBM)
    shapes = [
        (K, LA, ACB * BLK), (ACB, LA, BLK), (K * ACB, BLK),
        (7, COLS, BLK), (TRIPLES, OL, PADDED, BLK),
    ]
    halos = [
        (2, EARLY_ROWS, BLK), (4, 8, BLK), (2, EARLY_STRIP, BLK),
        (2, 4 * K, BLK), (4, 8, BLK), (2, LATE_STRIP, BLK),
    ]
    return pl.pallas_call(
        exchange_kernel,
        out_shape=[jax.ShapeDtypeStruct(s, F32) for s in shapes],
        in_specs=[hbm] * 7,
        out_specs=[vmem] * len(shapes),
        scratch_shapes=[
            pltpu.SMEM((3, SLOTS), jnp.int32),
            pltpu.VMEM((K, OL, OY, BLK), F32),
            pltpu.VMEM((3, OY, BLK), F32),
            pltpu.VMEM((WSL, BLK, BLK), F32),
            pltpu.VMEM((K, 8, ACB * BLK), F32),
            pltpu.VMEM((K, LA, ACB * BLK), F32),
            pltpu.VMEM((ACB, LA, LA), F32),
            pltpu.VMEM((OY, BLK), jnp.int32),
            pltpu.VMEM((ACB, LA, 2 * BLK), BF16),
            pltpu.VMEM((ACB, 2 * K, BLK), BF16),
            pltpu.VMEM((9, CAP, BLK), jnp.int32),
            pltpu.VMEM((9, CAP, BLK), jnp.int32),
            pltpu.VMEM((9, K * CAP, BLK), F32),
            pltpu.VMEM((9, K * CAP, BLK), F32),
            pltpu.VMEM((9, (K + 1) * CAP, BLK), F32),
            pltpu.VMEM((9, (K + 1) * CAP, BLK), F32),
            pltpu.VMEM((ACB, K + 8, BLK), F32),
            *[pltpu.VMEM(shape, F32) for shape in halos * 2],
            pltpu.SemaphoreType.DMA,
            pltpu.SemaphoreType.DMA,
            pltpu.SemaphoreType.DMA((6,)),
            pltpu.SemaphoreType.DMA((5,)),
            pltpu.SemaphoreType.DMA((5,)),
            pltpu.SemaphoreType.DMA((9,)),
        ],
        compiler_params=pltpu.CompilerParams(
            collective_id=0, has_side_effects=True, vmem_limit_bytes=30 * 2**20
        ),
        name="exchange",
    )(*(
        pltpu.with_memory_space_constraint(x, pltpu.HBM)
        for x in (inter, atm, mix, oc, vel, mask, weights)
    ))


def step_kernel(
    mixed, first_column, bottom, coef, state,
    atm_out, oc_out, atm_stage, oc_stage, work, shift, asem, osem,
):
    row = lax.broadcasted_iota(jnp.int32, (2 * BLK, 2 * BLK), 0) % BLK
    col = lax.broadcasted_iota(jnp.int32, (2 * BLK, 2 * BLK), 1)
    step = jnp.where(col < BLK, 1, BLK - 1)
    shift[...] = (row == (col + step) % BLK).astype(F32).astype(BF16)

    def ocean(t, carry):
        for n in range(3):
            k = jnp.minimum(3 * t + n, K - 1)
            surface = bottom[pl.ds(pl.multiple_of(k * ACB, ACB), ACB), :]
            for b in range(ACB):
                cols = slice(b * BLK, (b + 1) * BLK)
                atm_stage[3 * t + n, :, cols] = (
                    mixed[k, :, cols] + first_column[b] * surface[b:b + 1]
                )
        for sub in range(NSUB):
            def source(lev, start):
                if sub == 0:
                    return state[t, lev, start:start + 8, :]
                return work[(sub - 1) % 2, lev, start:start + 8, :]

            bottom_level = OL - 1
            whole = jnp.concatenate(
                [source(bottom_level, 8 + tile * 8) for tile in range(COLS // 8 + 1)], 0
            )
            shifted_by_product = sub % 2 == 1
            if shifted_by_product:
                moved = dot(jnp.concatenate(split2(whole), 1), shift[...])

            order = (
                [(tile, range(bottom_level)) for tile in range(COLS // 8)]
                + [(tile, [bottom_level]) for tile in range(COLS // 8)]
            ) if shifted_by_product else [(tile, range(OL)) for tile in range(COLS // 8)]
            for tile, levels in order:
                start = 8 + tile * 8
                c = [coef[n, tile * 8:tile * 8 + 8, :] for n in range(6)]
                x = {
                    lev: source(lev, start)
                    for lev in range(max(levels[0] - 1, 0), min(levels[-1] + 2, OL))
                }
                for lev in levels:
                    if lev == bottom_level and shifted_by_product:
                        north = moved[tile * 8:tile * 8 + 8, 0:BLK]
                        south = moved[tile * 8:tile * 8 + 8, BLK:2 * BLK]
                    else:
                        north = pltpu.roll(x[lev], BLK - 1, 1)
                        south = pltpu.roll(x[lev], 1, 1)
                    new = (
                        c[0] * source(lev, start + 1)
                        + c[1] * source(lev, start - 1)
                        + c[2] * north
                        + c[3] * south
                        + c[4] * (x[max(lev - 1, 0)] + x[min(lev + 1, OL - 1)])
                        + c[5] * x[lev]
                    )
                    work[sub % 2, lev, start:start + 8, :] = new
                    if tile == 0:
                        work[sub % 2, lev, 8 + COLS:PADDED, :] = new
                    if tile == COLS // 8 - 1:
                        work[sub % 2, lev, 0:8, :] = new
        for lev in range(OL):
            out = work[(NSUB - 1) % 2, lev, 8:8 + BLK, :].T
            for n in range(3):
                oc_stage[3 * t + n, lev] = out[n * LANES:n * LANES + OY]

        @pl.when(t < TRIPLES - 1)
        def _():
            three = pl.ds(3 * t, 3)
            pltpu.make_async_copy(atm_stage.at[three], atm_out.at[three], asem.at[t]).start()
            pltpu.make_async_copy(oc_stage.at[three], oc_out.at[three], osem.at[t]).start()

        return carry

    lax.fori_loop(0, TRIPLES, ocean, 0)
    copies = [
        pltpu.make_async_copy(stage.at[part], out.at[part], sem.at[TRIPLES - 1])
        for part in [pl.ds(K - 1, 1)]
        for stage, out, sem in ((atm_stage, atm_out, asem), (oc_stage, oc_out, osem))
    ]
    for copy in copies:
        copy.start()
    for t in range(TRIPLES - 1):
        three = pl.ds(3 * t, 3)
        pltpu.make_async_copy(atm_stage.at[three], atm_out.at[three], asem.at[t]).wait()
        pltpu.make_async_copy(oc_stage.at[three], oc_out.at[three], osem.at[t]).wait()
    for copy in copies:
        copy.wait()


def local_step(arrays):
    vmem = pl.BlockSpec(memory_space=pltpu.VMEM)
    hbm = pl.BlockSpec(memory_space=pltpu.HBM)
    return pl.pallas_call(
        step_kernel,
        out_shape=[
            jax.ShapeDtypeStruct((K, LA, ACB * BLK), F32),
            jax.ShapeDtypeStruct((K, OL, OY, BLK), F32),
        ],
        in_specs=[vmem] * len(arrays),
        out_specs=[hbm, hbm],
        scratch_shapes=[
            pltpu.VMEM((3 * TRIPLES, LA, ACB * BLK), F32),
            pltpu.VMEM((3 * TRIPLES, OL, OY, BLK), F32),
            pltpu.VMEM((2, OL, PADDED, BLK), F32),
            pltpu.VMEM((2 * BLK, 2 * BLK), BF16),
            pltpu.SemaphoreType.DMA((TRIPLES,)),
            pltpu.SemaphoreType.DMA((TRIPLES,)),
        ],
        compiler_params=pltpu.CompilerParams(vmem_limit_bytes=20 * 2**20),
        name="step",
    )(*arrays)


def body(atm, mix, oc, vel, mask, inter, weights):
    return tuple(local_step(exchange(inter, atm, mix, oc, vel, mask, weights)))


def solution(mesh):
    in_specs = (
        P(None, None, ("gx", "gy")),
        P(("gx", "gy"), None, None),
        P(None, None, "gy", "gx"),
        P(None, "gy", "gx"),
        P("gy", "gx"),
        P(None, ("gx", "gy")),
        P(("gx", "gy"), None, None),
    )
    out_specs = (P(None, None, ("gx", "gy")), P(None, None, "gy", "gx"))
    return jax.shard_map(body, mesh=mesh, in_specs=in_specs, out_specs=out_specs, check_vma=False)
```
